32 devices in a mesh: rep: 2 (over x), node: 2 (over core), local: 8 (over z, y).
Axes of the slice: x: 2, y: 2, z: 4, core: 2. Of those that a mesh axis runs over, the one named last changes fastest.
Arguments:
- tokens: bfloat16 [1024, 3584], P(('rep', 'node', 'local')), parts along dimension 0, may hold values from -6 to 6
- expert_ids: int32 [1024, 8], P(('rep', 'node', 'local')), parts along dimension 0, may hold values from 0 to 15, all different within a row; in each aligned block of 32 rows (0 to 31, 32 to 63, ...) at most 32 rows name the same one
- route_weights: bfloat16 [1024, 8], P(('rep', 'node', 'local')), parts along dimension 0, may hold values from 0.099609375 to 1
- w_up: bfloat16 [16, 3584, 1024], P(('node', 'local')), may hold values from -0.09375 to 0.09375
- w_down: bfloat16 [16, 1024, 3584], P(('node', 'local')), may hold values from -0.1875 to 0.1875
Outputs:
- mixed: bfloat16 [1024, 3584], P(('rep', 'node', 'local')), parts along dimension 0
The draws below stay inside these ranges and needn't reach their ends.
There are 2 independent parts, one for each index of `rep`. The reference program is written for one: setup_inputs(seed, part) draws one part's arguments, and reference() takes and returns one part's arrays. A program takes and returns all parts, laid end to end along the dimension named above; an argument that names none is the same for every part. Nothing has to cross between parts.
Inputs may be any that keep to these rules, and one draw needn't show every extreme that they name: `expert_ids`: the 8 experts of a token differ; in each aligned block of 32 rows (the rows of one device) no expert is named by more than 32 rows.
All inputs are finite; a program needn't handle non-finite values.
Results may differ from the reference program's by a relative error of at most 0.0058.
Values may be sent and summed in bfloat16 or wider, within the bound.
A program may use at most 64 MiB of HBM per device.

```python
import math
import jax
import jax.numpy as jnp
import numpy as np
from jax import lax

D = 3584
FF = 1024
TOP = 8
TOK_DEV = 32
EXPERTS = 16
MOST = 32
TOKENS = 512


def block_levels(key, shape, cuts, least, largest):
    loudness = 1.0
    for position, parts in cuts:
        steps = jax.random.uniform(jax.random.fold_in(jax.random.fold_in(key, 6), position), (parts,), jnp.float32, least / len(cuts), largest / len(cuts))
        loudness = loudness * jnp.repeat(jnp.exp(steps), shape[position] // parts).reshape((-1,) + (1,) * (len(shape) - 1 - position))
    return loudness


def shared_out(own_key, own, number, rows, amount, top, most, slope):
    order = jax.random.permutation(own_key, amount)
    packed, common = portions_of(amount, rows * top, most, slope, True), portions_of(amount, rows * top, most, slope, False)
    places = jnp.arange(amount)

    def named(tallies, rotation):
        used = int((tallies > 0).sum())
        fixed = max(1, used // 4)
        passed = fixed + (places - fixed + rotation * (used - fixed)) % max(1, amount - fixed)
        return jnp.zeros((amount,), jnp.int32).at[order[jnp.where(places < fixed, places, passed)]].set(jnp.asarray(tallies, jnp.int32))

    tallies = jnp.where(number % 4 == 0, named(packed, number // 4), named(common, number - number // 4 - 1))
    mixed = jax.random.permutation(jax.random.fold_in(own, 3), amount)
    donor, sink = mixed[0:amount // 2 * 2:2], mixed[1:amount // 2 * 2:2]
    slack = jnp.minimum(tallies[donor] - 1, most - tallies[sink]) // 2
    slack = jnp.where((donor == order[0]) | (sink == order[0]) | (tallies[sink] == 0), 0, jnp.maximum(slack, 0))
    passed = jax.random.randint(jax.random.fold_in(own, 4), (amount // 2,), 0, 1 << 20) % (slack + 1)
    tallies = tallies.at[donor].add(-passed).at[sink].add(passed)
    labels = jnp.searchsorted(jnp.cumsum(tallies), jnp.arange(rows * top), side="right").astype(jnp.int32)
    grid = labels.reshape(top, rows).T
    grid = grid[jax.random.permutation(jax.random.fold_in(own, 1), rows)]
    rotation = jax.random.randint(jax.random.fold_in(own, 2), (rows, 1), 0, top)
    return jnp.take_along_axis(grid, (jnp.arange(top)[None, :] + rotation) % top, axis=1)


def portions_of(number_of, total, reach, skew, full):
    portions = [(1 << 20) // math.isqrt(grade ** skew) + 1 for grade in range(1, number_of + 1)]
    largest = reach if full else min(reach, max(-(-total // number_of), total * portions[0] // sum(portions)))
    least = 1 if total - largest >= number_of - 1 else 0
    holding, rest = [largest] + [least] * (number_of - 1), total - largest - least * (number_of - 1)
    while rest > 0:
        candidates = [i for i in range(1, number_of) if holding[i] < largest] or [i for i in range(1, number_of) if holding[i] < reach]
        pool, remaining = sum([portions[i] for i in candidates]), rest
        for i in candidates:
            extra = min(reach - holding[i], max(1, remaining * portions[i] // pool), rest)
            holding[i] = holding[i] + extra
            rest = rest - extra
    return np.array(holding)


def bell_draw(own_key, shape, scale, most, split=(), kind=jnp.bfloat16):
    values = scale * jax.random.normal(own_key, shape, jnp.float32)
    if split:
        values = values * block_levels(own_key, shape, split, -0.22, 0.18)
    return jnp.clip(values, -most, most).astype(kind)


def setup_inputs(seed: int = 0, part: int = 0) -> dict:
    keys = jax.random.split(jax.random.key(seed), 6)
    own_keys = jax.random.split(jax.random.fold_in(keys[5], part), 6)
    tokens = bell_draw(own_keys[0], (TOKENS, D), 1.0, 6.0, ((0, 16),))
    expert_ids_keys = jax.random.split(jax.random.fold_in(own_keys[1], 1), TOKENS // TOK_DEV)
    expert_ids_turns = jax.random.permutation(jax.random.fold_in(own_keys[1], 3), TOKENS // TOK_DEV)
    expert_ids = jax.vmap(lambda own, number: shared_out(jax.random.fold_in(own_keys[1], 2), own, number, TOK_DEV, EXPERTS, TOP, MOST, 2))(expert_ids_keys, expert_ids_turns).reshape((TOKENS, TOP))
    route_weights = jnp.clip(0.099609375 + 0.9003906 * jax.random.uniform(own_keys[2], (TOKENS, TOP), jnp.float32) ** block_levels(own_keys[2], (TOKENS, TOP), ((0, 16),), -0.2, 0.2), 0.099609375, 1.0).astype(jnp.bfloat16)
    w_up = bell_draw(keys[3], (EXPERTS, D, FF), D ** -0.5, 0.09375, ((0, 16),))
    w_down = bell_draw(keys[4], (EXPERTS, FF, D), FF ** -0.5, 0.1875, ((0, 16),))
    return dict(tokens=tokens, expert_ids=expert_ids, route_weights=route_weights, w_up=w_up, w_down=w_down)


def reference(tokens, expert_ids, route_weights, w_up, w_down):
    total = tokens.shape[0]
    top = expert_ids.shape[1]
    flat_ids = expert_ids.reshape(-1)
    flat_weights = route_weights.reshape(-1).astype(jnp.float32)
    bound = EXPERTS * MOST
    filler = total * top

    def one_expert(carry, inputs):
        index, up, down = inputs
        picks = jnp.nonzero(flat_ids == index, size=bound, fill_value=filler)[0].astype(jnp.int32)
        valid = picks < filler
        token_rows = jnp.where(valid, picks // top, 0).astype(jnp.int32)
        rows = tokens[token_rows]
        hidden = jax.nn.silu(jnp.dot(rows, up, preferred_element_type=jnp.float32)).astype(jnp.bfloat16)
        answer = jnp.dot(hidden, down, preferred_element_type=jnp.float32).astype(jnp.bfloat16)
        scale = jnp.where(valid, flat_weights[jnp.minimum(picks, filler - 1)], 0.0)
        return carry.at[token_rows].add(scale[:, None] * answer.astype(jnp.float32)), None

    start = jnp.zeros((total, tokens.shape[1]), jnp.float32)
    result, _ = lax.scan(one_expert, start, (jnp.arange(EXPERTS, dtype=jnp.int32), w_up, w_down))
    return result.astype(jnp.bfloat16)
```

```python
import functools
import jax
import jax.numpy as jnp
from jax import lax
from jax.experimental import pallas as pl
from jax.experimental.pallas import tpu as pltpu
from jax.sharding import PartitionSpec as P

MESH = pl.DeviceIdType.MESH
LANES = 128
AHEAD_Z = 2
AHEAD_Y = 10
TABLE = 3
LAG_B = -2
LAG_A = (1, 1, 3)
LAG_P = (5, 6)
LAG_C = 7
LAG_E = 2
LAG_F = 5
LAG_G = 7
LAG_S = 9
LAG_FIN = 9
SWAP_G = ((),())
SWAP_R = ((),())


def moe_kernel(sizes, x_hbm, ids_ref, weights_ref, up_hbm, down_hbm, out_ref,
               xg, wg, up, down, acc, hid, psend, precv, pown, ysend, yrecv, zs, zr,
               own_sem, up_sem, down_sem,
               gz_s, gz_r, gy_s, gy_r, gp_s, gp_r,
               rp_s, rp_r, ry_s, ry_r, rz_s, rz_r):
    rows, major, chunks, width = sizes
    core = lax.axis_index("node")
    local = lax.axis_index("local")
    z, y = local // 2, lax.rem(local, 2)
    last = major - 1
    hr = rows // 2
    col = major * hr
    half = 2 * col
    grp = 2 * half
    nq = 2 * chunks
    f32 = jnp.float32

    up_z, down_z = jnp.minimum(z + 1, last), jnp.maximum(z - 1, 0)
    cross = lax.rem(z + 2, major)
    nexts = ({"local": up_z * 2 + y}, {"local": down_z * 2 + y}, {"local": cross * 2 + y})
    corner = (z == 0) | (z == last)
    far = last - z
    inward = {"local": jnp.where(z == 0, 1, last - 1) * 2 + y}
    outward = {"local": jnp.where(z == 1, 0, last) * 2 + y}
    at_y = {"local": z * 2 + (1 - y)}
    at_p = {"node": 1 - core}
    has = (z < last, z > 0, z >= 0)
    came = (z > 0, z < last, z >= 0, corner)
    block_of = (down_z, up_z, cross, far)

    barrier = pltpu.get_barrier_semaphore()
    peers = [{"local": lax.rem(z + d, major) * 2 + y} for d in range(1, major)] + [at_y, at_p]
    for peer in peers:
        pl.semaphore_signal(barrier, inc=1, device_id=peer, device_id_type=MESH)

    def zrow(zz):
        return pl.multiple_of(zz * hr, hr)

    own_x = []
    for h in range(2):
        own_x.append(pltpu.make_async_copy(
            x_hbm.at[pl.ds(h * hr, hr), :], xg.at[h, 0, pl.ds(zrow(z), hr), :], own_sem.at[h]))
        own_x[h].start()

    def cols(j):
        return pl.ds(pl.multiple_of(j * width, width), width)

    def up_copy(j):
        return pltpu.make_async_copy(up_hbm.at[0, cols(j), :], up.at[cols(j), :], up_sem.at[j])

    def down_copy(j):
        return pltpu.make_async_copy(down_hbm.at[0, :, cols(j)], down.at[:, cols(j)], down_sem.at[j])

    lax.fori_loop(0, chunks, lambda j, _: (up_copy(j).start(), 0)[1], 0)
    lax.fori_loop(0, chunks, lambda j, _: (down_copy(j).start(), 0)[1], 0)

    lanes = wg.shape[3]
    expert_row = lax.broadcasted_iota(jnp.int32, (lanes, rows), 0)
    spread = jnp.zeros((lanes, rows), f32)
    for k in range(ids_ref.shape[0]):
        spread += jnp.where(expert_row == ids_ref[k:k + 1, :], weights_ref[k:k + 1, :].astype(f32), 0.0)
    unit = (lax.broadcasted_iota(jnp.int32, (rows, rows), 0) == lax.broadcasted_iota(jnp.int32, (rows, rows), 1))
    table = lax.dot_general(
        unit.astype(f32).astype(jnp.bfloat16), spread.astype(jnp.bfloat16), (((1,), (1,)), ((), ())),
        preferred_element_type=f32).astype(wg.dtype)
    for h in range(2):
        wg[h, 0, pl.ds(zrow(z), hr), :] = table[h * hr:(h + 1) * hr, :]

    for h in range(2):
        own_x[h].wait()
    pl.semaphore_wait(barrier, len(peers))

    def split(q):
        h = (q >= chunks).astype(jnp.int32)
        return h, q - h * chunks

    def swapped(q, sets):
        if q is None:
            return jnp.bool_(False)
        out = jnp.bool_(False)
        for s in range(2):
            for k in sets[s]:
                out = out | (q == s * chunks + k)
        return out

    def count(sets):
        return len(sets[0]) + len(sets[1])

    def region(q, a, n, zz, size):
        if q is None:
            return wg.at[:, pl.ds(a, n), pl.ds(zrow(zz), size), :]
        h, j = split(q)
        return xg.at[h, pl.ds(a, n), pl.ds(zrow(zz), size), cols(j)]

    def idx(q):
        return nq if q is None else q

    def kind(q):
        return 1 if q is None else 0

    def remote(src, dst, s, r, device):
        return pltpu.make_async_remote_copy(
            src_ref=src, dst_ref=dst, send_sem=s, recv_sem=r, device_id=device, device_id_type=MESH)

    def sent(sem, ref):
        remote(ref, ref, sem, sem, at_p).wait_send()

    def gz(slot, n, q):
        v = region(q, 0, n, z, hr)
        return remote(v, v, gz_s.at[slot, kind(q)], gz_r.at[slot, idx(q)], nexts[slot])

    def relay(n, q):
        v = region(q, 0, n, cross, hr)
        return remote(v, v, gz_s.at[3, kind(q)], gz_r.at[3, idx(q)], outward)

    def gz_in(slot, n, q):
        v = region(q, 0, n, block_of[slot], hr)
        return remote(v, v, gz_s.at[slot, kind(q)], gz_r.at[slot, idx(q)], nexts[2])

    def gy(zz, q, own):
        return remote(region(q, 0, 1, zz, hr), region(q, 1, 1, zz, hr), gy_s.at[own, kind(q)], gy_r.at[idx(q)], at_y)

    def gy_in(zz, size, q):
        v = region(q, 1, 1, zz, size)
        return remote(v, v, gy_s.at[0, kind(q)], gy_r.at[idx(q)], at_y)

    def gp(k, q):
        return remote(region(q, k, 1, 0, col), region(q, 2 + k, 1, 0, col), gp_s.at[kind(q)], gp_r.at[idx(q)], at_p)

    def gp_in(q):
        v = region(q, 2, 2, 0, col)
        return remote(v, v, gp_s.at[kind(q)], gp_r.at[idx(q)], at_p)

    def plain(q, fn):
        if q is None:
            fn()
        else:
            pl.when(jnp.logical_not(swapped(q, SWAP_G)))(fn)

    def twice(q, fn):
        if q is not None and count(SWAP_G):
            pl.when(swapped(q, SWAP_G))(fn)

    def start_z(n, q):
        gz(2, n, q).start()
        for d in range(2):
            @pl.when(has[d])
            def _():
                gz(d, n, q).start()

    def stage0z(q):
        plain(q, lambda: start_z(1, q))

    def stage0y(q):
        gy(z, q, 1).start()

    def stage_b(q):
        def go():
            gy_in(z, hr, q).wait_recv()
            start_z(2, q)
        twice(q, go)

    def stage_a(slots, q):
        def step(n):
            for slot in slots:
                @pl.when(came[slot])
                def _():
                    gz_in(slot, n, q).wait_recv()
                    if slot == 2:
                        @pl.when(jnp.logical_not(corner))
                        def _():
                            relay(n, q).start()
                    if n == 1:
                        gy(block_of[slot], q, 0).start()
        plain(q, lambda: step(1))
        twice(q, lambda: step(2))

    def stage_p(k, q):
        if k == 1:
            plain(q, lambda: gy_in(0, col, q).wait_recv())
        gp(k, q).start()

    def stage_in(q):
        gp_in(q).wait_recv()

    expert = core * (2 * major) + local

    def stage_c(q):
        stage_in(q)
        h, j = split(q)

        @pl.when(h == 0)
        def _():
            up_copy(j).wait()
        x = xg[h, :, :, cols(j)].reshape(grp, width)
        part = jnp.dot(x, up[cols(j), :], preferred_element_type=f32)

        @pl.when(j == 0)
        def _():
            acc[...] = part

        @pl.when(j > 0)
        def _():
            acc[...] += part

        @pl.when(j == chunks - 1)
        def _():
            lane = lax.broadcasted_iota(jnp.int32, (grp, lanes), 1)
            table = wg[h].reshape(grp, lanes).astype(f32)
            weight = jnp.sum(jnp.where(lane == expert, table, 0.0), axis=1, keepdims=True)
            v = acc[...]
            hid[h] = (v / (1.0 + jnp.exp(-v)) * weight).astype(hid.dtype)

    def rp(r):
        h, j = split(r)
        return remote(psend.at[h, :, :, cols(j)], precv.at[h, :, :, cols(j)], rp_s.at[0], rp_r.at[r], at_p)

    def ry(size, r):
        h, j = split(r)
        return remote(ysend.at[h, pl.ds(0, size), cols(j)], yrecv.at[h, pl.ds(0, size), cols(j)],
                      ry_s.at[0], ry_r.at[r], at_y)

    def rz(slot, n, zz, r):
        h, j = split(r)
        return remote(zs.at[h, pl.ds(0, n), pl.ds(zrow(zz), hr), cols(j)],
                      zr.at[slot, h, pl.ds(0, n), :, cols(j)], rz_s.at[slot], rz_r.at[slot, r],
                      nexts[slot] if slot < 3 else inward)

    def plain_r(r, fn):
        pl.when(jnp.logical_not(swapped(r, SWAP_R)))(fn)

    def twice_r(r, fn):
        if count(SWAP_R):
            pl.when(swapped(r, SWAP_R))(fn)

    def stage_d(r):
        h, j = split(r)

        @pl.when(h == 0)
        def _():
            down_copy(j).wait()
        part = jnp.dot(hid[h], down[:, cols(j)], preferred_element_type=f32)
        psend[h, :, :, cols(j)] = part[half:, :].astype(psend.dtype).reshape(2, col, width)
        rp(r).start()
        pown[h, :, :, cols(j)] = part[:half, :].reshape(2, col, width)

    def stage_e(r):
        h, j = split(r)
        rp(r).wait_recv()

        def one():
            ysend[h, :, cols(j)] = (pown[h, 1, :, cols(j)] + precv[h, 1, :, cols(j)].astype(f32)).astype(ysend.dtype)
            ry(col, r).start()

        def two():
            pown[h, 1, :, cols(j)] += precv[h, 1, :, cols(j)].astype(f32)
        plain_r(r, one)
        twice_r(r, two)
        pown[h, 0, :, cols(j)] += precv[h, 0, :, cols(j)].astype(f32)

    def spread_z(m, r):
        h, j = split(r)
        v = (h, pl.ds(0, m), slice(None), cols(j))
        zs[v] = pown[v].astype(zs.dtype)

        @pl.when(corner)
        def _():
            rz(3, m, far, r).start()
            rz(2, m, cross, r).start()
        for slot in range(2):
            @pl.when(has[slot])
            def _():
                rz(slot, m, (up_z, down_z)[slot], r).start()

    def stage_f(r):
        h, j = split(r)

        def one():
            ry(col, r).wait_recv()
            pown[h, 0, :, cols(j)] += yrecv[h, :, cols(j)].astype(f32)
            spread_z(1, r)
        plain_r(r, one)
        twice_r(r, lambda: spread_z(2, r))

    def stage_g(r):
        h, j = split(r)

        def flow(m):
            rz(3, m, cross, r).wait_recv()
            v = (h, pl.ds(0, m), pl.ds(zrow(cross), hr), cols(j))
            zs[v] = (pown[v] + zr[3, h, pl.ds(0, m), :, cols(j)].astype(f32)).astype(zs.dtype)
            rz(2, m, cross, r).start()

        @pl.when(jnp.logical_not(corner))
        def _():
            plain_r(r, lambda: flow(1))
            twice_r(r, lambda: flow(2))

    def settle(m, r):
        h, j = split(r)
        v = (h, pl.ds(0, m), pl.ds(zrow(z), hr), cols(j))
        for slot in range(3):
            @pl.when(came[slot])
            def _():
                rz(slot, m, z, r).wait_recv()
                pown[v] += zr[slot, h, pl.ds(0, m), :, cols(j)].astype(f32)

    def stage_s(r):
        h, j = split(r)
        mine = pl.ds(zrow(z), hr)

        def two():
            settle(2, r)
            ysend[h, pl.ds(0, hr), cols(j)] = pown[h, 1, mine, cols(j)].astype(ysend.dtype)
            ry(hr, r).start()
        plain_r(r, lambda: settle(1, r))
        twice_r(r, two)

    def stage_fin(r):
        h, j = split(r)
        mine = pl.ds(zrow(z), hr)
        out = pl.ds(pl.multiple_of(h * hr, hr), hr)

        def one():
            out_ref[out, cols(j)] = pown[h, 0, mine, cols(j)].astype(out_ref.dtype)

        def two():
            ry(hr, r).wait_recv()
            out_ref[out, cols(j)] = (
                pown[h, 0, mine, cols(j)] + yrecv[h, pl.ds(0, hr), cols(j)].astype(f32)).astype(out_ref.dtype)
        plain_r(r, one)
        twice_r(r, two)

    gather = [(stage_b, LAG_B)]
    gather += [(functools.partial(stage_a, s), lag) for s, lag in zip(((0, 1), (2,), (3,)), LAG_A)]
    gather += [(functools.partial(stage_p, k), LAG_P[k]) for k in range(2)]
    start_r = LAG_C + chunks - 1
    reduce_a = [(stage_e, start_r + LAG_E), (stage_f, start_r + LAG_F), (stage_g, start_r + LAG_G),
                (stage_s, start_r + LAG_S), (stage_fin, start_r + LAG_FIN)]
    late = start_r + LAG_FIN

    def run(t, stages):
        for fn, lag in stages:
            @pl.when((t >= lag) & (t < nq + lag))
            def _():
                fn(t - lag)

    def early(t):
        @pl.when(t + AHEAD_Z < nq)
        def _():
            stage0z(t + AHEAD_Z)

        @pl.when(t + AHEAD_Y < nq)
        def _():
            stage0y(t + AHEAD_Y)
        for fn, lag in gather[1:] + [(stage_in, LAG_C)]:
            @pl.when(t == TABLE + lag)
            def _():
                fn(None)
        run(t, gather)

    def first(t, _):
        early(t)
        run(t, [(stage_c, LAG_C)])
        return 0

    def middle(t, _):
        early(t)
        run(t, reduce_a)
        run(t, [(stage_c, LAG_C), (stage_d, start_r)])
        return 0

    def final(t, _):
        run(t, reduce_a)
        run(t, [(stage_d, start_r)])
        return 0

    lax.fori_loop(0, AHEAD_Z, lambda q, _: (stage0z(q), 0)[1], 0)
    lax.fori_loop(0, AHEAD_Y, lambda q, _: (stage0y(q), 0)[1], 0)
    stage0z(None)
    stage0y(None)
    lax.fori_loop(0, start_r, first, 0)
    lax.fori_loop(start_r, nq + LAG_C, middle, 0)
    lax.fori_loop(nq + LAG_C, nq + late, final, 0)

    def whole(sem, blocks):
        while blocks:
            n = min(blocks, 4 * chunks)
            r = n if n < 4 else n - n % 4
            if n < 4:
                ref = xg.at[0, pl.ds(0, 1), pl.ds(0, hr), pl.ds(0, n * width)]
            else:
                ref = xg.at[0, pl.ds(0, 1), pl.ds(0, col), pl.ds(0, r // 4 * width)]
            sent(sem, ref)
            blocks -= r

    ng, nr = count(SWAP_G), count(SWAP_R)
    whole(gy_s.at[1, 0], nq)
    whole(gy_s.at[0, 0], (nq - ng) * last)
    whole(gp_s.at[0], nq * 2 * major)
    for slot in range(4):
        @pl.when((*has, jnp.logical_not(corner))[slot])
        def _():
            whole(gz_s.at[slot, 0], nq + ng)
            sent(gz_s.at[slot, 1], wg.at[:, pl.ds(0, 1), pl.ds(0, hr), :])
    sent(gy_s.at[1, 1], wg.at[:, pl.ds(0, 1), pl.ds(0, hr), :])
    sent(gy_s.at[0, 1], wg.at[:, pl.ds(0, 1), pl.ds(0, last * hr), :])
    sent(gp_s.at[1], wg.at[:, pl.ds(0, 2), pl.ds(0, col), :])
    whole(rp_s.at[0], nq * 2 * major)
    whole(ry_s.at[0], (nq - nr) * major + nr)
    for slot in range(4):
        @pl.when((*has, corner)[slot])
        def _():
            whole(rz_s.at[slot], nq + nr)


def fused(tokens, expert_ids, route_weights, w_up, w_down, width=512):
    rows, depth = tokens.shape
    ff = w_up.shape[2]
    experts = lax.axis_size(("node", "local"))
    major = lax.axis_size("local") // 2
    chunks = depth // width
    lanes = -(-experts // LANES) * LANES
    col = major * rows // 2
    bf, f32 = jnp.bfloat16, jnp.float32
    nq = 2 * chunks
    dma = pltpu.SemaphoreType.DMA
    return pl.pallas_call(
        functools.partial(moe_kernel, (rows, major, chunks, width)),
        out_shape=pltpu.VMEM((rows, depth), bf),
        in_specs=[
            pl.BlockSpec(memory_space=pl.ANY),
            pl.BlockSpec(memory_space=pltpu.VMEM),
            pl.BlockSpec(memory_space=pltpu.VMEM),
            pl.BlockSpec(memory_space=pl.ANY),
            pl.BlockSpec(memory_space=pl.ANY),
        ],
        out_specs=pl.BlockSpec(memory_space=pltpu.VMEM),
        scratch_shapes=[
            pltpu.VMEM((2, 4, col, depth), bf),
            pltpu.VMEM((2, 4, col, lanes), bf),
            pltpu.VMEM((depth, ff), bf),
            pltpu.VMEM((ff, depth), bf),
            pltpu.VMEM((4 * col, ff), f32),
            pltpu.VMEM((2, 4 * col, ff), bf),
            pltpu.VMEM((2, 2, col, depth), bf),
            pltpu.VMEM((2, 2, col, depth), bf),
            pltpu.VMEM((2, 2, col, depth), f32),
            pltpu.VMEM((2, col, depth), bf),
            pltpu.VMEM((2, col, depth), bf),
            pltpu.VMEM((2, 2, col, depth), bf),
            pltpu.VMEM((4, 2, 2, rows // 2, depth), bf),
            dma((2,)), dma((chunks,)), dma((chunks,)),
            dma((4, 2)), dma((4, nq + 1)),
            dma((2, 2)), dma((nq + 1,)),
            dma((2,)), dma((nq + 1,)),
            dma((1,)), dma((nq,)),
            dma((1,)), dma((nq,)),
            dma((4,)), dma((4, nq)),
        ],
        compiler_params=pltpu.CompilerParams(
            collective_id=0, has_side_effects=True, vmem_limit_bytes=60 * 1024 * 1024),
    )(tokens, expert_ids.T, route_weights.T, w_up, w_down)


def place_rows(targets, groups, width):
    onehot = (targets[:, None] == jnp.arange(groups, dtype=jnp.int32)[None, :]).astype(jnp.int32)
    before = jnp.cumsum(onehot, axis=0) - onehot
    rank = jnp.sum(before * onehot, axis=1)
    return jnp.where(targets >= 0, targets * width + rank, groups * width)


def per_device(tokens, expert_ids, route_weights, w_up, w_down):
    up_matrix = w_up[0]
    down_matrix = w_down[0]
    rows = tokens.shape[0]
    top = expert_ids.shape[1]
    width_d = tokens.shape[1]
    experts = lax.axis_size(("node", "local"))
    most = max(4, 2 * rows * top // experts)
    slot = place_rows(expert_ids.reshape(-1), experts, most)
    source = tokens[jnp.arange(rows * top, dtype=jnp.int32) // top]
    buffer = jnp.zeros((experts * most, width_d), jnp.bfloat16).at[slot].set(source, mode="drop")
    buffer = buffer.reshape(experts, most, width_d)
    received = lax.all_to_all(buffer, ("node", "local"), split_axis=0, concat_axis=0, tiled=True)
    shape = received.shape
    flat = received.reshape(-1, shape[-1])
    hidden = jax.nn.silu(jnp.dot(flat, up_matrix, preferred_element_type=jnp.float32)).astype(
        jnp.bfloat16
    )
    answer = jnp.dot(hidden, down_matrix, preferred_element_type=jnp.float32).astype(jnp.bfloat16)
    done = answer.reshape(shape)
    returned = lax.all_to_all(
        done, ("node", "local"), split_axis=0, concat_axis=0, tiled=True
    ).reshape(experts * most, width_d)
    picked = returned[jnp.minimum(slot, experts * most - 1)].reshape(rows, top, width_d)
    mixed = jnp.einsum("tk,tkd->td", route_weights, picked, preferred_element_type=jnp.float32)
    return mixed.astype(jnp.bfloat16)


def solution(mesh):
    placed = (
        P(("rep", "node", "local"), None),
        P(("rep", "node", "local"), None),
        P(("rep", "node", "local"), None),
        P(("node", "local"), None, None),
        P(("node", "local"), None, None),
    )

    def body(tokens, expert_ids, route_weights, w_up, w_down):
        experts = mesh.shape["node"] * mesh.shape["local"]
        near_dense = experts <= 2 * expert_ids.shape[1]
        if near_dense and mesh.shape["node"] == 2 and mesh.shape["local"] == 8:
            return fused(tokens, expert_ids, route_weights, w_up, w_down)
        return per_device(tokens, expert_ids, route_weights, w_up, w_down)

    return jax.shard_map(
        body,
        mesh=mesh,
        in_specs=placed,
        out_specs=P(("rep", "node", "local"), None),
        check_vma=False,
    )
```

```python
import functools
import jax
import jax.numpy as jnp
from jax import lax
from jax.experimental import pallas as pl
from jax.experimental.pallas import tpu as pltpu
from jax.sharding import PartitionSpec as P

MESH = pl.DeviceIdType.MESH
LANES = 128
AHEAD_Z = 2
AHEAD_Y = 10
TABLE = 3
LAG_A = (1, 1, 3)
LAG_P = (5, 6)
LAG_C = 7
LAG_E = 2
LAG_F = 5
LAG_G = 8
LAG_S = 11
DEFER = 10
DIRECT = 3


def moe_kernel(sizes, x_hbm, ids_ref, weights_ref, up_hbm, down_hbm, out_ref,
               xg, wg, up, down, acc, hid, psend, precv, pown, ysend, yrecv, zs, zr,
               own_sem, up_sem, down_sem,
               gz_s, gz_r, gy_s, gy_r, gp_s, gp_r,
               rp_s, rp_r, ry_s, ry_r, ro_s, ro_r, rz_s, rz_r):
    rows, major, chunks, width = sizes
    core = lax.axis_index("node")
    local = lax.axis_index("local")
    z, y = local // 2, lax.rem(local, 2)
    last = major - 1
    hr = rows // 2
    col = major * hr
    half = 2 * col
    grp = 2 * half
    nq = 2 * chunks
    f32 = jnp.float32

    up_z, down_z = jnp.minimum(z + 1, last), jnp.maximum(z - 1, 0)
    cross = lax.rem(z + 2, major)
    corner = (z == 0) | (z == last)
    far = jnp.where(corner, last - z, cross)
    nexts = tuple({"local": zz * 2 + y} for zz in (up_z, down_z, cross, far))
    inward = {"local": jnp.where(z == 0, 1, last - 1) * 2 + y}
    outward = {"local": jnp.where(z == 1, 0, last) * 2 + y}
    at_y = {"local": z * 2 + (1 - y)}
    at_p = {"node": 1 - core}
    has = (z < last, z > 0, z >= 0)
    came = (z > 0, z < last, z >= 0, corner)
    from_rel = (last, 1, 2, jnp.where(z == 0, last, 1))
    to_rel = (1, last, 2, jnp.where(z == 0, last, 1))
    relay_rel = jnp.where(z == 1, last, 1)

    barrier = pltpu.get_barrier_semaphore()
    peers = [{"local": lax.rem(z + d, major) * 2 + y} for d in range(1, major)] + [at_y, at_p]
    for peer in peers:
        pl.semaphore_signal(barrier, inc=1, device_id=peer, device_id_type=MESH)

    def rel(k, n=1):
        return pl.ds(k * hr if isinstance(k, int) else pl.multiple_of(k * hr, hr), n * hr)

    own_x = []
    for h in range(2):
        own_x.append(pltpu.make_async_copy(
            x_hbm.at[pl.ds(h * hr, hr), :], xg.at[h, 0, rel(0), :], own_sem.at[h]))
        own_x[h].start()

    def cols(j):
        return pl.ds(pl.multiple_of(j * width, width), width)

    def up_copy(j):
        return pltpu.make_async_copy(up_hbm.at[0, cols(j), :], up.at[cols(j), :], up_sem.at[j])

    def down_copy(j):
        return pltpu.make_async_copy(down_hbm.at[0, :, cols(j)], down.at[:, cols(j)], down_sem.at[j])

    lax.fori_loop(0, chunks, lambda j, _: (up_copy(j).start(), 0)[1], 0)
    lax.fori_loop(0, chunks, lambda j, _: (down_copy(j).start(), 0)[1], 0)

    pl.semaphore_wait(barrier, len(peers))

    def split(q):
        h = (q >= chunks).astype(jnp.int32)
        return h, q - h * chunks

    def region(q, a, n, k, m):
        if q is None:
            return wg.at[:, pl.ds(a, n), rel(k, m), :]
        h, j = split(q)
        return xg.at[h, pl.ds(a, n), rel(k, m), cols(j)]

    def idx(q):
        return nq if q is None else q

    def kind(q):
        return 1 if q is None else 0

    def remote(src, dst, s, r, device):
        return pltpu.make_async_remote_copy(
            src_ref=src, dst_ref=dst, send_sem=s, recv_sem=r, device_id=device, device_id_type=MESH)

    def sent(sem, ref):
        remote(ref, ref, sem, sem, at_p).wait_send()

    def own(q, a, k):
        if q is None:
            return wg.at[:, 0, rel(0), :], wg.at[:, a, rel(k), :]
        h, j = split(q)
        return x_hbm.at[pl.ds(pl.multiple_of(h * hr, hr), hr), cols(j)], xg.at[h, a, rel(k), cols(j)]

    def gz(slot, q):
        return remote(*own(q, 0, from_rel[slot]), gz_s.at[slot, kind(q)], gz_r.at[slot, idx(q)], nexts[slot])

    def relay(q):
        return remote(region(q, 0, 1, 2, 1), region(q, 0, 1, relay_rel, 1),
                      gz_s.at[3, kind(q)], gz_r.at[3, idx(q)], outward)

    def gz_in(slot, q):
        v = region(q, 0, 1, from_rel[slot], 1)
        return remote(v, v, gz_s.at[slot, kind(q)], gz_r.at[slot, idx(q)], nexts[2])

    def gy(k, q):
        v = own(q, 1, 0) if k is None else (region(q, 0, 1, k, 1), region(q, 1, 1, k, 1))
        return remote(*v, gy_s.at[int(k is None), kind(q)], gy_r.at[idx(q)], at_y)

    def gy_in(q):
        v = region(q, 1, 1, 0, major)
        return remote(v, v, gy_s.at[0, kind(q)], gy_r.at[idx(q)], at_y)

    def gp(k, q):
        return remote(region(q, k, 1, 0, major), region(q, 2 + k, 1, 0, major), gp_s.at[kind(q)], gp_r.at[idx(q)], at_p)

    def gp_in(q):
        v = region(q, 2, 2, 0, major)
        return remote(v, v, gp_s.at[kind(q)], gp_r.at[idx(q)], at_p)

    def stage0z(q):
        gz(2, q).start()
        for d in range(2):
            @pl.when(has[d])
            def _():
                gz(d, q).start()

    def stage0y(q):
        gy(None, q).start()

    def stage_a(slots, q):
        for slot in slots:
            @pl.when(came[slot])
            def _():
                gz_in(slot, q).wait_recv()
                if slot == 2:
                    @pl.when(jnp.logical_not(corner))
                    def _():
                        relay(q).start()
                gy(from_rel[slot], q).start()

    def stage_p(k, q):
        if k == 1:
            gy_in(q).wait_recv()
        gp(k, q).start()

    def stage_in(q):
        gp_in(q).wait_recv()

    lanes = wg.shape[3]
    expert = core * (2 * major) + local

    def stage_c(q):
        stage_in(q)
        h, j = split(q)

        @pl.when(h == 0)
        def _():
            up_copy(j).wait()
        x = xg[h, :, :, cols(j)].reshape(grp, width)
        part = jnp.dot(x, up[cols(j), :], preferred_element_type=f32)

        @pl.when(j == 0)
        def _():
            acc[...] = part

        @pl.when(j > 0)
        def _():
            acc[...] += part

        @pl.when(j == chunks - 1)
        def _():
            lane = lax.broadcasted_iota(jnp.int32, (grp, lanes), 1)
            table = wg[h].reshape(grp, lanes).astype(f32)
            weight = jnp.sum(jnp.where(lane == expert, table, 0.0), axis=1, keepdims=True)
            v = acc[...]
            hid[h] = (v / (1.0 + jnp.exp(-v)) * weight).astype(hid.dtype)

    def rp(r):
        h, j = split(r)
        return remote(psend.at[h, :, :, cols(j)], precv.at[h, :, :, cols(j)], rp_s.at[0], rp_r.at[r], at_p)

    def ry(r):
        h, j = split(r)
        v = (h, rel(1, last), cols(j))
        return remote(ysend.at[v], yrecv.at[v], ry_s.at[0], ry_r.at[r], at_y)

    def ro(r):
        h, j = split(r)
        v = (h, rel(0), cols(j))
        return remote(ysend.at[v], yrecv.at[v], ro_s.at[0], ro_r.at[r], at_y)

    def rz(slot, r):
        h, j = split(r)
        return remote(zs.at[h, rel(to_rel[slot]), cols(j)], zr.at[slot, h, :, cols(j)],
                      rz_s.at[slot], rz_r.at[slot, r], nexts[slot])

    def rr(r):
        h, j = split(r)
        return remote(zs.at[h, rel(to_rel[3]), cols(j)], zr.at[3, h, :, cols(j)], rz_s.at[3], rz_r.at[3, r], inward)

    def stage_d(r):
        h, j = split(r)

        @pl.when(h == 0)
        def _():
            down_copy(j).wait()
        part = jnp.dot(hid[h], down[:, cols(j)], preferred_element_type=f32)
        psend[h, :, :, cols(j)] = part[half:, :].astype(psend.dtype).reshape(2, col, width)
        rp(r).start()
        pown[h, :, :, cols(j)] = part[:half, :].reshape(2, col, width)

    def stage_e(r):
        h, j = split(r)
        rp(r).wait_recv()
        ysend[h, :, cols(j)] = (pown[h, 1, :, cols(j)] + precv[h, 1, :, cols(j)].astype(f32)).astype(ysend.dtype)
        ry(r).start()

        @pl.when(r < nq - DEFER)
        def _():
            ro(r).start()
        pown[h, 0, :, cols(j)] += precv[h, 0, :, cols(j)].astype(f32)

        @pl.when(r == nq - 1)
        def _():
            lax.fori_loop(nq - DEFER, nq, lambda k, _: (ro(k).start(), 0)[1], 0)

    def stage_f(r):
        h, j = split(r)
        ry(r).wait_recv()
        v = (h, rel(1, last), cols(j))
        zs[v] = (pown[h, 0, rel(1, last), cols(j)] + yrecv[v].astype(f32)).astype(zs.dtype)

        by_hand = r < nq - DIRECT

        @pl.when(corner & by_hand)
        def _():
            rr(r).start()

        @pl.when(corner & jnp.logical_not(by_hand))
        def _():
            rz(3, r).start()

        @pl.when(corner | jnp.logical_not(by_hand))
        def _():
            rz(2, r).start()
        for slot in range(2):
            @pl.when(has[slot])
            def _():
                rz(slot, r).start()

    def stage_g(r):
        h, j = split(r)

        @pl.when(jnp.logical_not(corner))
        def _():
            rr(r).wait_recv()
            v = (h, rel(2), cols(j))
            zs[v] = (pown[h, 0, rel(2), cols(j)] + yrecv[v].astype(f32) + zr[3, h, :, cols(j)].astype(f32)).astype(zs.dtype)
            rz(2, r).start()

    def stage_s(r):
        h, j = split(r)
        ro(r).wait_recv()
        v = (h, 0, rel(0), cols(j))
        pown[v] += yrecv[h, rel(0), cols(j)].astype(f32)
        for slot in range(4):
            @pl.when(came[slot] & (r >= nq - DIRECT) if slot == 3 else came[slot])
            def _():
                rz(slot, r).wait_recv()
                pown[v] += zr[slot, h, :, cols(j)].astype(f32)
        out_ref[pl.ds(pl.multiple_of(h * hr, hr), hr), cols(j)] = pown[v].astype(out_ref.dtype)

    gather = [(functools.partial(stage_a, s), lag) for s, lag in zip(((0, 1), (2,), (3,)), LAG_A)]
    gather += [(functools.partial(stage_p, k), LAG_P[k]) for k in range(2)]
    start_r = LAG_C + chunks - 1
    reduce_a = [(stage_e, start_r + LAG_E), (stage_f, start_r + LAG_F)]
    late = start_r + max(LAG_F, LAG_G - DIRECT, LAG_S - DEFER)
    early_rows = nq - DEFER

    def run(t, stages):
        for fn, lag in stages:
            @pl.when((t >= lag) & (t < nq + lag))
            def _():
                fn(t - lag)

    def early(t):
        @pl.when(t + AHEAD_Z < nq)
        def _():
            stage0z(t + AHEAD_Z)

        @pl.when(t + AHEAD_Y < nq)
        def _():
            stage0y(t + AHEAD_Y)
        for fn, lag in gather + [(stage_in, LAG_C)]:
            @pl.when(t == TABLE + lag)
            def _():
                fn(None)
        run(t, gather)

    def back(t):
        run(t, reduce_a)

        @pl.when((t >= start_r + LAG_G) & (t < nq - DIRECT + start_r + LAG_G))
        def _():
            stage_g(t - start_r - LAG_G)

        @pl.when((t >= start_r + LAG_S) & (t < early_rows + start_r + LAG_S))
        def _():
            stage_s(t - start_r - LAG_S)

    def first(t, _):
        early(t)
        run(t, [(stage_c, LAG_C)])
        return 0

    def middle(t, _):
        early(t)
        back(t)
        run(t, [(stage_c, LAG_C), (stage_d, start_r)])
        return 0

    def final(t, _):
        back(t)
        run(t, [(stage_d, start_r)])
        return 0

    lax.fori_loop(0, AHEAD_Z, lambda q, _: (stage0z(q), 0)[1], 0)
    lax.fori_loop(0, AHEAD_Y, lambda q, _: (stage0y(q), 0)[1], 0)
    expert_row = lax.broadcasted_iota(jnp.int32, (lanes, rows), 0)
    spread = jnp.zeros((lanes, rows), f32)
    for k in range(ids_ref.shape[0]):
        spread += jnp.where(expert_row == ids_ref[k:k + 1, :], weights_ref[k:k + 1, :].astype(f32), 0.0)
    unit = (lax.broadcasted_iota(jnp.int32, (rows, rows), 0) == lax.broadcasted_iota(jnp.int32, (rows, rows), 1))
    table = lax.dot_general(
        unit.astype(f32).astype(jnp.bfloat16), spread.astype(jnp.bfloat16), (((1,), (1,)), ((), ())),
        preferred_element_type=f32).astype(wg.dtype)
    for h in range(2):
        wg[h, 0, rel(0), :] = table[h * hr:(h + 1) * hr, :]

    stage0z(None)
    stage0y(None)
    for h in range(2):
        own_x[h].wait()
    lax.fori_loop(0, start_r, first, 0)
    lax.fori_loop(start_r, nq + LAG_C, middle, 0)
    lax.fori_loop(nq + LAG_C, nq + late, final, 0)

    def whole(sem, blocks):
        while blocks:
            n = min(blocks, 4 * chunks)
            r = n if n < 4 else n - n % 4
            if n < 4:
                ref = xg.at[0, pl.ds(0, 1), pl.ds(0, hr), pl.ds(0, n * width)]
            else:
                ref = xg.at[0, pl.ds(0, 1), pl.ds(0, col), pl.ds(0, r // 4 * width)]
            sent(sem, ref)
            blocks -= r

    whole(gy_s.at[1, 0], nq)
    whole(gy_s.at[0, 0], nq * last)
    whole(gp_s.at[0], nq * 2 * major)
    for slot in range(4):
        @pl.when((*has, jnp.logical_not(corner))[slot])
        def _():
            whole(gz_s.at[slot, 0], nq)
            sent(gz_s.at[slot, 1], wg.at[:, 0, rel(0), :])
    sent(gy_s.at[1, 1], wg.at[:, 0, rel(0), :])
    sent(gy_s.at[0, 1], wg.at[:, 0, rel(1, last), :])
    sent(gp_s.at[1], wg.at[:, pl.ds(0, 2), :, :])
    whole(rp_s.at[0], nq * 2 * major)
    whole(ry_s.at[0], nq * last)
    lax.fori_loop(early_rows, nq, lambda r, _: (stage_s(r), 0)[1], 0)
    whole(ro_s.at[0], nq)
    for slot in range(4):
        @pl.when((*has, corner)[slot])
        def _():
            whole(rz_s.at[slot], nq)


def fused(tokens, expert_ids, route_weights, w_up, w_down, width=512):
    rows, depth = tokens.shape
    ff = w_up.shape[2]
    experts = lax.axis_size(("node", "local"))
    major = lax.axis_size("local") // 2
    chunks = depth // width
    lanes = -(-experts // LANES) * LANES
    col = major * rows // 2
    bf, f32 = jnp.bfloat16, jnp.float32
    nq = 2 * chunks
    dma = pltpu.SemaphoreType.DMA
    return pl.pallas_call(
        functools.partial(moe_kernel, (rows, major, chunks, width)),
        out_shape=pltpu.VMEM((rows, depth), bf),
        in_specs=[
            pl.BlockSpec(memory_space=pl.ANY),
            pl.BlockSpec(memory_space=pltpu.VMEM),
            pl.BlockSpec(memory_space=pltpu.VMEM),
            pl.BlockSpec(memory_space=pl.ANY),
            pl.BlockSpec(memory_space=pl.ANY),
        ],
        out_specs=pl.BlockSpec(memory_space=pltpu.VMEM),
        scratch_shapes=[
            pltpu.VMEM((2, 4, col, depth), bf),
            pltpu.VMEM((2, 4, col, lanes), bf),
            pltpu.VMEM((depth, ff), bf),
            pltpu.VMEM((ff, depth), bf),
            pltpu.VMEM((4 * col, ff), f32),
            pltpu.VMEM((2, 4 * col, ff), bf),
            pltpu.VMEM((2, 2, col, depth), bf),
            pltpu.VMEM((2, 2, col, depth), bf),
            pltpu.VMEM((2, 2, col, depth), f32),
            pltpu.VMEM((2, col, depth), bf),
            pltpu.VMEM((2, col, depth), bf),
            pltpu.VMEM((2, col, depth), bf),
            pltpu.VMEM((4, 2, rows // 2, depth), bf),
            dma((2,)), dma((chunks,)), dma((chunks,)),
            dma((4, 2)), dma((4, nq + 1)),
            dma((2, 2)), dma((nq + 1,)),
            dma((2,)), dma((nq + 1,)),
            dma((1,)), dma((nq,)),
            dma((1,)), dma((nq,)),
            dma((1,)), dma((nq,)),
            dma((4,)), dma((4, nq)),
        ],
        compiler_params=pltpu.CompilerParams(
            collective_id=0, has_side_effects=True, vmem_limit_bytes=60 * 1024 * 1024),
    )(tokens, expert_ids.T, route_weights.T, w_up, w_down)


def place_rows(targets, groups, width):
    onehot = (targets[:, None] == jnp.arange(groups, dtype=jnp.int32)[None, :]).astype(jnp.int32)
    before = jnp.cumsum(onehot, axis=0) - onehot
    rank = jnp.sum(before * onehot, axis=1)
    return jnp.where(targets >= 0, targets * width + rank, groups * width)


def per_device(tokens, expert_ids, route_weights, w_up, w_down):
    up_matrix = w_up[0]
    down_matrix = w_down[0]
    rows = tokens.shape[0]
    top = expert_ids.shape[1]
    width_d = tokens.shape[1]
    experts = lax.axis_size(("node", "local"))
    most = max(4, 2 * rows * top // experts)
    slot = place_rows(expert_ids.reshape(-1), experts, most)
    source = tokens[jnp.arange(rows * top, dtype=jnp.int32) // top]
    buffer = jnp.zeros((experts * most, width_d), jnp.bfloat16).at[slot].set(source, mode="drop")
    buffer = buffer.reshape(experts, most, width_d)
    received = lax.all_to_all(buffer, ("node", "local"), split_axis=0, concat_axis=0, tiled=True)
    shape = received.shape
    flat = received.reshape(-1, shape[-1])
    hidden = jax.nn.silu(jnp.dot(flat, up_matrix, preferred_element_type=jnp.float32)).astype(
        jnp.bfloat16
    )
    answer = jnp.dot(hidden, down_matrix, preferred_element_type=jnp.float32).astype(jnp.bfloat16)
    done = answer.reshape(shape)
    returned = lax.all_to_all(
        done, ("node", "local"), split_axis=0, concat_axis=0, tiled=True
    ).reshape(experts * most, width_d)
    picked = returned[jnp.minimum(slot, experts * most - 1)].reshape(rows, top, width_d)
    mixed = jnp.einsum("tk,tkd->td", route_weights, picked, preferred_element_type=jnp.float32)
    return mixed.astype(jnp.bfloat16)


def solution(mesh):
    placed = (
        P(("rep", "node", "local"), None),
        P(("rep", "node", "local"), None),
        P(("rep", "node", "local"), None),
        P(("node", "local"), None, None),
        P(("node", "local"), None, None),
    )

    def body(tokens, expert_ids, route_weights, w_up, w_down):
        experts = mesh.shape["node"] * mesh.shape["local"]
        near_dense = experts <= 2 * expert_ids.shape[1]
        if near_dense and mesh.shape["node"] == 2 and mesh.shape["local"] == 8:
            return fused(tokens, expert_ids, route_weights, w_up, w_down)
        return per_device(tokens, expert_ids, route_weights, w_up, w_down)

    return jax.shard_map(
        body,
        mesh=mesh,
        in_specs=placed,
        out_specs=P(("rep", "node", "local"), None),
        check_vma=False,
    )
```

```python
import functools
import jax
import jax.numpy as jnp
from jax import lax
from jax.experimental import pallas as pl
from jax.experimental.pallas import tpu as pltpu
from jax.sharding import PartitionSpec as P

MESH = pl.DeviceIdType.MESH
LANES = 128
AHEAD_Z = 2
AHEAD_Y = 7
TABLE = 3
LAG_A = (1, 1, 3)
LAG_P = (5, 6)
LAG_C = 7
LAG_E = 2
LAG_F = 5
LAG_G = 8
LAG_S = 11
DEFER = 14
DIRECT = 2


def moe_kernel(sizes, x_hbm, ids_ref, weights_ref, up_hbm, down_hbm, out_ref,
               xg, wg, up, down, acc, hid, psend, precv, pown, ysend, yrecv, zs, zr,
               own_sem, up_sem, down_sem,
               gz_s, gz_r, gy_s, gy_r, gp_s, gp_r,
               rp_s, rp_r, ry_s, ry_r, ro_s, ro_r, rz_s, rz_r):
    rows, major, chunks, width = sizes
    core = lax.axis_index("node")
    local = lax.axis_index("local")
    z, y = local // 2, lax.rem(local, 2)
    last = major - 1
    hr = rows // 2
    col = major * hr
    half = 2 * col
    grp = 2 * half
    nq = 2 * chunks
    f32 = jnp.float32

    up_z, down_z = jnp.minimum(z + 1, last), jnp.maximum(z - 1, 0)
    cross = lax.rem(z + 2, major)
    corner = (z == 0) | (z == last)
    far = jnp.where(corner, last - z, cross)
    nexts = tuple({"local": zz * 2 + y} for zz in (up_z, down_z, cross, far))
    inward = {"local": jnp.where(z == 0, 1, last - 1) * 2 + y}
    outward = {"local": jnp.where(z == 1, 0, last) * 2 + y}
    at_y = {"local": z * 2 + (1 - y)}
    at_p = {"node": 1 - core}
    has = (z < last, z > 0, z >= 0)
    came = (z > 0, z < last, z >= 0, corner)
    from_rel = (last, 1, 2, jnp.where(z == 0, last, 1))
    to_rel = (1, last, 2, jnp.where(z == 0, last, 1))
    relay_rel = jnp.where(z == 1, last, 1)

    barrier = pltpu.get_barrier_semaphore()
    peers = [{"local": lax.rem(z + d, major) * 2 + y} for d in range(1, major)] + [at_y, at_p]
    for peer in peers:
        pl.semaphore_signal(barrier, inc=1, device_id=peer, device_id_type=MESH)

    def rel(k, n=1):
        return pl.ds(k * hr if isinstance(k, int) else pl.multiple_of(k * hr, hr), n * hr)

    own_x = []
    for h in range(2):
        own_x.append(pltpu.make_async_copy(
            x_hbm.at[pl.ds(h * hr, hr), :], xg.at[h, 0, rel(0), :], own_sem.at[h]))
        own_x[h].start()

    def cols(j):
        return pl.ds(pl.multiple_of(j * width, width), width)

    def up_copy(j):
        return pltpu.make_async_copy(up_hbm.at[0, cols(j), :], up.at[cols(j), :], up_sem.at[j])

    def down_copy(j):
        return pltpu.make_async_copy(down_hbm.at[0, :, cols(j)], down.at[:, cols(j)], down_sem.at[j])

    pl.semaphore_wait(barrier, len(peers))

    def split(q):
        h = (q >= chunks).astype(jnp.int32)
        return h, q - h * chunks

    def region(q, a, n, k, m):
        if q is None:
            return wg.at[:, pl.ds(a, n), rel(k, m), :]
        h, j = split(q)
        return xg.at[h, pl.ds(a, n), rel(k, m), cols(j)]

    def idx(q):
        return nq if q is None else q

    def kind(q):
        return 1 if q is None else 0

    def remote(src, dst, s, r, device):
        return pltpu.make_async_remote_copy(
            src_ref=src, dst_ref=dst, send_sem=s, recv_sem=r, device_id=device, device_id_type=MESH)

    def sent(sem, ref):
        remote(ref, ref, sem, sem, at_p).wait_send()

    def own(q, a, k):
        if q is None:
            return wg.at[:, 0, rel(0), :], wg.at[:, a, rel(k), :]
        h, j = split(q)
        return x_hbm.at[pl.ds(pl.multiple_of(h * hr, hr), hr), cols(j)], xg.at[h, a, rel(k), cols(j)]

    def gz(slot, q):
        return remote(*own(q, 0, from_rel[slot]), gz_s.at[slot, kind(q)], gz_r.at[slot, idx(q)], nexts[slot])

    def relay(q):
        return remote(region(q, 0, 1, 2, 1), region(q, 0, 1, relay_rel, 1),
                      gz_s.at[3, kind(q)], gz_r.at[3, idx(q)], outward)

    def gz_in(slot, q):
        v = region(q, 0, 1, from_rel[slot], 1)
        return remote(v, v, gz_s.at[slot, kind(q)], gz_r.at[slot, idx(q)], nexts[2])

    def gy(k, q):
        v = own(q, 1, 0) if k is None else (region(q, 0, 1, k, 1), region(q, 1, 1, k, 1))
        return remote(*v, gy_s.at[int(k is None), kind(q)], gy_r.at[idx(q)], at_y)

    def gy_in(q):
        v = region(q, 1, 1, 0, major)
        return remote(v, v, gy_s.at[0, kind(q)], gy_r.at[idx(q)], at_y)

    def gp(k, q):
        return remote(region(q, k, 1, 0, major), region(q, 2 + k, 1, 0, major), gp_s.at[kind(q)], gp_r.at[idx(q)], at_p)

    def gp_in(q):
        v = region(q, 2, 2, 0, major)
        return remote(v, v, gp_s.at[kind(q)], gp_r.at[idx(q)], at_p)

    def stage0z(q):
        gz(2, q).start()
        for d in range(2):
            @pl.when(has[d])
            def _():
                gz(d, q).start()

    def stage0y(q):
        gy(None, q).start()

    def stage_a(slots, q):
        for slot in slots:
            @pl.when(came[slot])
            def _():
                gz_in(slot, q).wait_recv()
                if slot == 2:
                    @pl.when(jnp.logical_not(corner))
                    def _():
                        relay(q).start()
                gy(from_rel[slot], q).start()

    def stage_p(k, q):
        if k == 1:
            gy_in(q).wait_recv()
        gp(k, q).start()

    def stage_in(q):
        gp_in(q).wait_recv()

    lanes = wg.shape[3]
    expert = core * (2 * major) + local

    def stage_c(q):
        stage_in(q)
        h, j = split(q)

        @pl.when(h == 0)
        def _():
            up_copy(j).wait()
        x = xg[h, :, :, cols(j)].reshape(grp, width)
        part = jnp.dot(x, up[cols(j), :], preferred_element_type=f32)

        @pl.when(j == 0)
        def _():
            acc[...] = part

        @pl.when(j > 0)
        def _():
            acc[...] += part

        @pl.when(j == chunks - 1)
        def _():
            lane = lax.broadcasted_iota(jnp.int32, (grp, lanes), 1)
            table = wg[h].reshape(grp, lanes).astype(f32)
            weight = jnp.sum(jnp.where(lane == expert, table, 0.0), axis=1, keepdims=True)
            v = acc[...]
            hid[h] = (v / (1.0 + jnp.exp(-v)) * weight).astype(hid.dtype)

    def rp(r):
        h, j = split(r)
        return remote(psend.at[h, :, :, cols(j)], precv.at[h, :, :, cols(j)], rp_s.at[0], rp_r.at[r], at_p)

    def ry(r):
        h, j = split(r)
        v = (h, rel(1, last), cols(j))
        return remote(ysend.at[v], yrecv.at[v], ry_s.at[0], ry_r.at[r], at_y)

    def ro(r):
        h, j = split(r)
        v = (h, rel(0), cols(j))
        return remote(ysend.at[v], yrecv.at[v], ro_s.at[0], ro_r.at[r], at_y)

    def rz(slot, r):
        h, j = split(r)
        return remote(zs.at[h, rel(to_rel[slot]), cols(j)], zr.at[slot, h, :, cols(j)],
                      rz_s.at[slot], rz_r.at[slot, r], nexts[slot])

    def rr(r):
        h, j = split(r)
        return remote(zs.at[h, rel(to_rel[3]), cols(j)], zr.at[3, h, :, cols(j)], rz_s.at[3], rz_r.at[3, r], inward)

    def stage_d(r):
        h, j = split(r)

        @pl.when(h == 0)
        def _():
            down_copy(j).wait()
        part = jnp.dot(hid[h], down[:, cols(j)], preferred_element_type=f32)
        psend[h, :, :, cols(j)] = part[half:, :].astype(psend.dtype).reshape(2, col, width)
        rp(r).start()
        pown[h, :, :, cols(j)] = part[:half, :].reshape(2, col, width)

    def stage_e(r):
        h, j = split(r)
        rp(r).wait_recv()
        ysend[h, :, cols(j)] = (pown[h, 1, :, cols(j)] + precv[h, 1, :, cols(j)].astype(f32)).astype(ysend.dtype)
        ry(r).start()

        @pl.when(r < nq - DEFER)
        def _():
            ro(r).start()
        pown[h, 0, :, cols(j)] += precv[h, 0, :, cols(j)].astype(f32)

        @pl.when(r == nq - 1)
        def _():
            lax.fori_loop(nq - DEFER, nq, lambda k, _: (ro(k).start(), 0)[1], 0)

    def stage_f(r):
        h, j = split(r)
        ry(r).wait_recv()
        v = (h, rel(1, last), cols(j))
        zs[v] = (pown[h, 0, rel(1, last), cols(j)] + yrecv[v].astype(f32)).astype(zs.dtype)

        by_hand = r < nq - DIRECT

        @pl.when(corner & by_hand)
        def _():
            rr(r).start()

        @pl.when(corner & jnp.logical_not(by_hand))
        def _():
            rz(3, r).start()

        @pl.when(corner | jnp.logical_not(by_hand))
        def _():
            rz(2, r).start()
        for slot in range(2):
            @pl.when(has[slot])
            def _():
                rz(slot, r).start()

    def stage_g(r):
        h, j = split(r)

        @pl.when(jnp.logical_not(corner))
        def _():
            rr(r).wait_recv()
            v = (h, rel(2), cols(j))
            zs[v] = (pown[h, 0, rel(2), cols(j)] + yrecv[v].astype(f32) + zr[3, h, :, cols(j)].astype(f32)).astype(zs.dtype)
            rz(2, r).start()

    def stage_s(r):
        h, j = split(r)
        ro(r).wait_recv()
        v = (h, 0, rel(0), cols(j))
        pown[v] += yrecv[h, rel(0), cols(j)].astype(f32)
        for slot in range(4):
            @pl.when(came[slot] & (r >= nq - DIRECT) if slot == 3 else came[slot])
            def _():
                rz(slot, r).wait_recv()
                pown[v] += zr[slot, h, :, cols(j)].astype(f32)
        out_ref[pl.ds(pl.multiple_of(h * hr, hr), hr), cols(j)] = pown[v].astype(out_ref.dtype)

    gather = [(functools.partial(stage_a, s), lag) for s, lag in zip(((0, 1), (2,), (3,)), LAG_A)]
    gather += [(functools.partial(stage_p, k), LAG_P[k]) for k in range(2)]
    start_r = LAG_C + chunks - 1
    reduce_a = [(stage_e, start_r + LAG_E), (stage_f, start_r + LAG_F)]
    late = start_r + max(LAG_F, LAG_G - DIRECT, LAG_S - DEFER)
    early_rows = nq - DEFER

    def run(t, stages):
        for fn, lag in stages:
            @pl.when((t >= lag) & (t < nq + lag))
            def _():
                fn(t - lag)

    def early(t):
        @pl.when(t + AHEAD_Z < nq)
        def _():
            stage0z(t + AHEAD_Z)

        @pl.when(t + AHEAD_Y < nq)
        def _():
            stage0y(t + AHEAD_Y)
        for fn, lag in gather + [(stage_in, LAG_C)]:
            @pl.when(t == TABLE + lag)
            def _():
                fn(None)
        run(t, gather)

    def back(t):
        run(t, reduce_a)

        @pl.when((t >= start_r + LAG_G) & (t < nq - DIRECT + start_r + LAG_G))
        def _():
            stage_g(t - start_r - LAG_G)

        @pl.when((t >= start_r + LAG_S) & (t < early_rows + start_r + LAG_S))
        def _():
            stage_s(t - start_r - LAG_S)

    def first(t, _):
        @pl.when(t < chunks)
        def _():
            up_copy(t).start()
            down_copy(t).start()
        early(t)
        run(t, [(stage_c, LAG_C)])
        return 0

    def middle(t, _):
        early(t)
        back(t)
        run(t, [(stage_c, LAG_C), (stage_d, start_r)])
        return 0

    def final(t, _):
        back(t)
        run(t, [(stage_d, start_r)])
        return 0

    lax.fori_loop(0, AHEAD_Z, lambda q, _: (stage0z(q), 0)[1], 0)
    lax.fori_loop(0, AHEAD_Y, lambda q, _: (stage0y(q), 0)[1], 0)
    expert_row = lax.broadcasted_iota(jnp.int32, (lanes, rows), 0)
    spread = jnp.zeros((lanes, rows), f32)
    for k in range(ids_ref.shape[0]):
        spread += jnp.where(expert_row == ids_ref[k:k + 1, :], weights_ref[k:k + 1, :].astype(f32), 0.0)
    unit = (lax.broadcasted_iota(jnp.int32, (rows, rows), 0) == lax.broadcasted_iota(jnp.int32, (rows, rows), 1))
    table = lax.dot_general(
        unit.astype(f32).astype(jnp.bfloat16), spread.astype(jnp.bfloat16), (((1,), (1,)), ((), ())),
        preferred_element_type=f32).astype(wg.dtype)
    for h in range(2):
        wg[h, 0, rel(0), :] = table[h * hr:(h + 1) * hr, :]

    stage0z(None)
    stage0y(None)
    for h in range(2):
        own_x[h].wait()
    lax.fori_loop(0, start_r, first, 0)
    lax.fori_loop(start_r, nq + LAG_C, middle, 0)
    lax.fori_loop(nq + LAG_C, nq + late, final, 0)

    def whole(sem, blocks):
        while blocks:
            n = min(blocks, 4 * chunks)
            r = n if n < 4 else n - n % 4
            if n < 4:
                ref = xg.at[0, pl.ds(0, 1), pl.ds(0, hr), pl.ds(0, n * width)]
            else:
                ref = xg.at[0, pl.ds(0, 1), pl.ds(0, col), pl.ds(0, r // 4 * width)]
            sent(sem, ref)
            blocks -= r

    whole(gy_s.at[1, 0], nq)
    whole(gy_s.at[0, 0], nq * last)
    whole(gp_s.at[0], nq * 2 * major)
    for slot in range(4):
        @pl.when((*has, jnp.logical_not(corner))[slot])
        def _():
            whole(gz_s.at[slot, 0], nq)
            sent(gz_s.at[slot, 1], wg.at[:, 0, rel(0), :])
    sent(gy_s.at[1, 1], wg.at[:, 0, rel(0), :])
    sent(gy_s.at[0, 1], wg.at[:, 0, rel(1, last), :])
    sent(gp_s.at[1], wg.at[:, pl.ds(0, 2), :, :])
    whole(rp_s.at[0], nq * 2 * major)
    whole(ry_s.at[0], nq * last)
    lax.fori_loop(early_rows, nq, lambda r, _: (stage_s(r), 0)[1], 0)
    whole(ro_s.at[0], nq)
    for slot in range(4):
        @pl.when((*has, corner)[slot])
        def _():
            whole(rz_s.at[slot], nq)


def fused(tokens, expert_ids, route_weights, w_up, w_down, width=512):
    rows, depth = tokens.shape
    ff = w_up.shape[2]
    experts = lax.axis_size(("node", "local"))
    major = lax.axis_size("local") // 2
    chunks = depth // width
    lanes = -(-experts // LANES) * LANES
    col = major * rows // 2
    bf, f32 = jnp.bfloat16, jnp.float32
    nq = 2 * chunks
    dma = pltpu.SemaphoreType.DMA
    return pl.pallas_call(
        functools.partial(moe_kernel, (rows, major, chunks, width)),
        out_shape=pltpu.VMEM((rows, depth), bf),
        in_specs=[
            pl.BlockSpec(memory_space=pl.ANY),
            pl.BlockSpec(memory_space=pltpu.VMEM),
            pl.BlockSpec(memory_space=pltpu.VMEM),
            pl.BlockSpec(memory_space=pl.ANY),
            pl.BlockSpec(memory_space=pl.ANY),
        ],
        out_specs=pl.BlockSpec(memory_space=pltpu.VMEM),
        scratch_shapes=[
            pltpu.VMEM((2, 4, col, depth), bf),
            pltpu.VMEM((2, 4, col, lanes), bf),
            pltpu.VMEM((depth, ff), bf),
            pltpu.VMEM((ff, depth), bf),
            pltpu.VMEM((4 * col, ff), f32),
            pltpu.VMEM((2, 4 * col, ff), bf),
            pltpu.VMEM((2, 2, col, depth), bf),
            pltpu.VMEM((2, 2, col, depth), bf),
            pltpu.VMEM((2, 2, col, depth), f32),
            pltpu.VMEM((2, col, depth), bf),
            pltpu.VMEM((2, col, depth), bf),
            pltpu.VMEM((2, col, depth), bf),
            pltpu.VMEM((4, 2, rows // 2, depth), bf),
            dma((2,)), dma((chunks,)), dma((chunks,)),
            dma((4, 2)), dma((4, nq + 1)),
            dma((2, 2)), dma((nq + 1,)),
            dma((2,)), dma((nq + 1,)),
            dma((1,)), dma((nq,)),
            dma((1,)), dma((nq,)),
            dma((1,)), dma((nq,)),
            dma((4,)), dma((4, nq)),
        ],
        compiler_params=pltpu.CompilerParams(
            collective_id=0, has_side_effects=True, vmem_limit_bytes=60 * 1024 * 1024),
    )(tokens, expert_ids.T, route_weights.T, w_up, w_down)


def place_rows(targets, groups, width):
    onehot = (targets[:, None] == jnp.arange(groups, dtype=jnp.int32)[None, :]).astype(jnp.int32)
    before = jnp.cumsum(onehot, axis=0) - onehot
    rank = jnp.sum(before * onehot, axis=1)
    return jnp.where(targets >= 0, targets * width + rank, groups * width)


def per_device(tokens, expert_ids, route_weights, w_up, w_down):
    up_matrix = w_up[0]
    down_matrix = w_down[0]
    rows = tokens.shape[0]
    top = expert_ids.shape[1]
    width_d = tokens.shape[1]
    experts = lax.axis_size(("node", "local"))
    most = max(4, 2 * rows * top // experts)
    slot = place_rows(expert_ids.reshape(-1), experts, most)
    source = tokens[jnp.arange(rows * top, dtype=jnp.int32) // top]
    buffer = jnp.zeros((experts * most, width_d), jnp.bfloat16).at[slot].set(source, mode="drop")
    buffer = buffer.reshape(experts, most, width_d)
    received = lax.all_to_all(buffer, ("node", "local"), split_axis=0, concat_axis=0, tiled=True)
    shape = received.shape
    flat = received.reshape(-1, shape[-1])
    hidden = jax.nn.silu(jnp.dot(flat, up_matrix, preferred_element_type=jnp.float32)).astype(
        jnp.bfloat16
    )
    answer = jnp.dot(hidden, down_matrix, preferred_element_type=jnp.float32).astype(jnp.bfloat16)
    done = answer.reshape(shape)
    returned = lax.all_to_all(
        done, ("node", "local"), split_axis=0, concat_axis=0, tiled=True
    ).reshape(experts * most, width_d)
    picked = returned[jnp.minimum(slot, experts * most - 1)].reshape(rows, top, width_d)
    mixed = jnp.einsum("tk,tkd->td", route_weights, picked, preferred_element_type=jnp.float32)
    return mixed.astype(jnp.bfloat16)


def solution(mesh):
    placed = (
        P(("rep", "node", "local"), None),
        P(("rep", "node", "local"), None),
        P(("rep", "node", "local"), None),
        P(("node", "local"), None, None),
        P(("node", "local"), None, None),
    )

    def body(tokens, expert_ids, route_weights, w_up, w_down):
        experts = mesh.shape["node"] * mesh.shape["local"]
        near_dense = experts <= 2 * expert_ids.shape[1]
        if near_dense and mesh.shape["node"] == 2 and mesh.shape["local"] == 8:
            return fused(tokens, expert_ids, route_weights, w_up, w_down)
        return per_device(tokens, expert_ids, route_weights, w_up, w_down)

    return jax.shard_map(
        body,
        mesh=mesh,
        in_specs=placed,
        out_specs=P(("rep", "node", "local"), None),
        check_vma=False,
    )
```

```python
import functools
import jax
import jax.numpy as jnp
from jax import lax
from jax.experimental import pallas as pl
from jax.experimental.pallas import tpu as pltpu
from jax.sharding import PartitionSpec as P

MESH = pl.DeviceIdType.MESH
LANES = 128
AHEAD_Z = 2
AHEAD_Y = 7
TABLE = 3
LAG_A = (1, 1, 3)
LAG_P = (4, 6)
LAG_C = 7
LAG_E = 2
LAG_F = 5
LAG_G = 8
LAG_S = 11
DEFER = 14
DIRECT = 2


def moe_kernel(sizes, x_hbm, ids_ref, weights_ref, up_hbm, down_hbm, out_ref,
               xg, wg, up, down, acc, hid, psend, precv, pown, ysend, yrecv, zs, zr,
               own_sem, up_sem,
               gz_s, gz_r, gy_s, gy_r, gp_s, gp_r,
               rp_s, rp_r, ry_s, ry_r, ro_s, ro_r, rz_s, rz_r):
    rows, major, chunks, width = sizes
    core = lax.axis_index("node")
    local = lax.axis_index("local")
    z, y = local // 2, lax.rem(local, 2)
    last = major - 1
    hr = rows // 2
    col = major * hr
    half = 2 * col
    grp = 2 * half
    nq = 2 * chunks
    f32 = jnp.float32

    up_z, down_z = jnp.minimum(z + 1, last), jnp.maximum(z - 1, 0)
    cross = lax.rem(z + 2, major)
    corner = (z == 0) | (z == last)
    far = jnp.where(corner, last - z, cross)
    nexts = tuple({"local": zz * 2 + y} for zz in (up_z, down_z, cross, far))
    inward = {"local": jnp.where(z == 0, 1, last - 1) * 2 + y}
    outward = {"local": jnp.where(z == 1, 0, last) * 2 + y}
    at_y = {"local": z * 2 + (1 - y)}
    at_p = {"node": 1 - core}
    has = (z < last, z > 0, z >= 0)
    came = (z > 0, z < last, z >= 0, corner)
    from_rel = (last, 1, 2, jnp.where(z == 0, last, 1))
    to_rel = (1, last, 2, jnp.where(z == 0, last, 1))
    lane_of = (0, 0, 1, 2)
    relay_rel = jnp.where(z == 1, last, 1)

    barrier = pltpu.get_barrier_semaphore()
    peers = [{"local": lax.rem(z + d, major) * 2 + y} for d in range(1, major)] + [at_y, at_p]
    for peer in peers:
        pl.semaphore_signal(barrier, inc=1, device_id=peer, device_id_type=MESH)

    def rel(k, n=1):
        return pl.ds(k * hr if isinstance(k, int) else pl.multiple_of(k * hr, hr), n * hr)

    own_x = []
    for h in range(2):
        own_x.append(pltpu.make_async_copy(
            x_hbm.at[pl.ds(h * hr, hr), :], xg.at[h, 0, rel(0), :], own_sem.at[h]))
        own_x[h].start()

    def cols(j):
        return pl.ds(pl.multiple_of(j * width, width), width)

    def up_copy(j):
        return pltpu.make_async_copy(up_hbm.at[0, cols(j), :], up.at[cols(j), :], up_sem.at[j])

    def down_copy(j):
        return pltpu.make_async_copy(down_hbm.at[0, :, cols(j)], down.at[:, cols(j)], up_sem.at[j])

    pl.semaphore_wait(barrier, len(peers))

    def split(q):
        h = (q >= chunks).astype(jnp.int32)
        return h, q - h * chunks

    def region(q, a, n, k, m):
        if q is None:
            return wg.at[:, pl.ds(a, n), rel(k, m), :]
        h, j = split(q)
        return xg.at[h, pl.ds(a, n), rel(k, m), cols(j)]

    def idx(q):
        return nq if q is None else q

    def kind(q):
        return 1 if q is None else 0

    def remote(src, dst, s, r, device):
        return pltpu.make_async_remote_copy(
            src_ref=src, dst_ref=dst, send_sem=s, recv_sem=r, device_id=device, device_id_type=MESH)

    def sent(sem, ref):
        remote(ref, ref, sem, sem, at_p).wait_send()

    def own(q, a, k):
        if q is None:
            return wg.at[:, 0, rel(0), :], wg.at[:, a, rel(k), :]
        h, j = split(q)
        return x_hbm.at[pl.ds(pl.multiple_of(h * hr, hr), hr), cols(j)], xg.at[h, a, rel(k), cols(j)]

    def gz(slot, q):
        return remote(*own(q, 0, from_rel[slot]), gz_s.at[slot, kind(q)], gz_r.at[lane_of[slot], idx(q)], nexts[slot])

    def relay(q):
        return remote(region(q, 0, 1, 2, 1), region(q, 0, 1, relay_rel, 1),
                      gz_s.at[3, kind(q)], gz_r.at[2, idx(q)], outward)

    def gz_in(lane, blocks, q):
        v = region(q, 0, 1, (1, 2, from_rel[3])[lane], blocks)
        return remote(v, v, gz_s.at[2, kind(q)], gz_r.at[lane, idx(q)], nexts[2])

    def gy(k, q):
        v = own(q, 1, 0) if k is None else (region(q, 0, 1, k, 1), region(q, 1, 1, k, 1))
        return remote(*v, gy_s.at[int(k is None), kind(q)], gy_r.at[idx(q)], at_y)

    def gy_in(q):
        v = region(q, 1, 1, 0, major)
        return remote(v, v, gy_s.at[0, kind(q)], gy_r.at[idx(q)], at_y)

    def gp(k, q):
        return remote(region(q, k, 1, 0, major), region(q, 2 + k, 1, 0, major), gp_s.at[kind(q)], gp_r.at[idx(q)], at_p)

    def gp_in(q):
        v = region(q, 2, 2, 0, major)
        return remote(v, v, gp_s.at[kind(q)], gp_r.at[idx(q)], at_p)

    def stage0z(q):
        gz(2, q).start()
        for d in range(2):
            @pl.when(has[d])
            def _():
                gz(d, q).start()

    def stage0y(q):
        gy(None, q).start()

    def stage_a(lane, q):
        if lane == 0:
            @pl.when(corner)
            def _():
                gz_in(0, 1, q).wait_recv()
                gy(jnp.where(z == 0, 1, last), q).start()

            @pl.when(jnp.logical_not(corner))
            def _():
                gz_in(0, 2, q).wait_recv()
                gy(1, q).start()
                gy(last, q).start()
        elif lane == 1:
            gz_in(1, 1, q).wait_recv()

            @pl.when(jnp.logical_not(corner))
            def _():
                relay(q).start()
            gy(2, q).start()
        else:
            @pl.when(corner)
            def _():
                gz_in(2, 1, q).wait_recv()
                gy(from_rel[3], q).start()

    def stage_p(k, q):
        if k == 1:
            gy_in(q).wait_recv()
        gp(k, q).start()

    def stage_in(q):
        gp_in(q).wait_recv()

    lanes = wg.shape[3]
    expert = core * (2 * major) + local

    def stage_c(q):
        stage_in(q)
        h, j = split(q)

        @pl.when(h == 0)
        def _():
            both = up.at[pl.ds(0, 2 * width), :]
            pltpu.make_async_copy(both, both, up_sem.at[j]).wait()
        x = xg[h, :, :, cols(j)].reshape(grp, width)
        part = jnp.dot(x, up[cols(j), :], preferred_element_type=f32)

        @pl.when(j == 0)
        def _():
            acc[...] = part

        @pl.when(j > 0)
        def _():
            acc[...] += part

        @pl.when(j == chunks - 1)
        def _():
            lane = lax.broadcasted_iota(jnp.int32, (grp, lanes), 1)
            table = wg[h].reshape(grp, lanes).astype(f32)
            weight = jnp.sum(jnp.where(lane == expert, table, 0.0), axis=1, keepdims=True)
            v = acc[...]
            hid[h] = (v / (1.0 + jnp.exp(-v)) * weight).astype(hid.dtype)

    def rp(r):
        h, j = split(r)
        return remote(psend.at[h, :, :, cols(j)], precv.at[h, :, :, cols(j)], rp_s.at[0], rp_r.at[r], at_p)

    def ry(r):
        h, j = split(r)
        v = (h, rel(1, last), cols(j))
        return remote(ysend.at[v], yrecv.at[v], ry_s.at[0], ry_r.at[r], at_y)

    def ro(r):
        h, j = split(r)
        v = (h, rel(0), cols(j))
        return remote(ysend.at[v], yrecv.at[v], ro_s.at[0], ro_r.at[r], at_y)

    def rz(slot, r):
        h, j = split(r)
        return remote(zs.at[h, rel(to_rel[slot]), cols(j)], zr.at[slot, h, :, cols(j)],
                      rz_s.at[slot], rz_r.at[0, r], nexts[slot])

    def rr(r):
        h, j = split(r)
        return remote(zs.at[h, rel(to_rel[3]), cols(j)], zr.at[3, h, :, cols(j)], rz_s.at[3], rz_r.at[1, r], inward)

    def stage_d(r):
        h, j = split(r)

        part = jnp.dot(hid[h], down[:, cols(j)], preferred_element_type=f32)
        psend[h, :, :, cols(j)] = part[half:, :].astype(psend.dtype).reshape(2, col, width)
        rp(r).start()
        pown[h, :, :, cols(j)] = part[:half, :].reshape(2, col, width)

    def stage_e(r):
        h, j = split(r)
        rp(r).wait_recv()
        ysend[h, :, cols(j)] = (pown[h, 1, :, cols(j)] + precv[h, 1, :, cols(j)].astype(f32)).astype(ysend.dtype)
        ry(r).start()

        @pl.when(r < nq - DEFER)
        def _():
            ro(r).start()
        pown[h, 0, :, cols(j)] += precv[h, 0, :, cols(j)].astype(f32)

        @pl.when(r == nq - 1)
        def _():
            lax.fori_loop(nq - DEFER, nq, lambda k, _: (ro(k).start(), 0)[1], 0)

    def stage_f(r):
        h, j = split(r)
        ry(r).wait_recv()
        v = (h, rel(1, last), cols(j))
        zs[v] = (pown[h, 0, rel(1, last), cols(j)] + yrecv[v].astype(f32)).astype(zs.dtype)

        by_hand = r < nq - DIRECT

        @pl.when(corner & by_hand)
        def _():
            rr(r).start()

        @pl.when(corner & jnp.logical_not(by_hand))
        def _():
            rz(3, r).start()

        @pl.when(corner | jnp.logical_not(by_hand))
        def _():
            rz(2, r).start()
        for slot in range(2):
            @pl.when(has[slot])
            def _():
                rz(slot, r).start()

    def stage_g(r):
        h, j = split(r)

        @pl.when(jnp.logical_not(corner))
        def _():
            rr(r).wait_recv()
            v = (h, rel(2), cols(j))
            zs[v] = (pown[h, 0, rel(2), cols(j)] + yrecv[v].astype(f32) + zr[3, h, :, cols(j)].astype(f32)).astype(zs.dtype)
            rz(2, r).start()

    def stage_s(r):
        h, j = split(r)
        ro(r).wait_recv()
        v = (h, 0, rel(0), cols(j))
        pown[v] += yrecv[h, rel(0), cols(j)].astype(f32)
        def arrived(n):
            blocks = zr.at[pl.ds(0, n), h, :, cols(j)]
            remote(blocks, blocks, rz_s.at[0], rz_r.at[0, r], nexts[2]).wait_recv()

        two = corner & (r < nq - DIRECT)
        pl.when(two)(lambda: arrived(2))
        pl.when(jnp.logical_not(two))(lambda: arrived(3))
        for slot in range(4):
            @pl.when(came[slot] & (r >= nq - DIRECT) if slot == 3 else came[slot])
            def _():
                pown[v] += zr[slot, h, :, cols(j)].astype(f32)
        out_ref[pl.ds(pl.multiple_of(h * hr, hr), hr), cols(j)] = pown[v].astype(out_ref.dtype)

    gather = [(functools.partial(stage_a, s), lag) for s, lag in zip(range(3), LAG_A)]
    gather += [(functools.partial(stage_p, k), LAG_P[k]) for k in range(2)]
    start_r = LAG_C + chunks - 1
    reduce_a = [(stage_e, start_r + LAG_E), (stage_f, start_r + LAG_F)]
    late = start_r + max(LAG_F, LAG_G - DIRECT, LAG_S - DEFER)
    early_rows = nq - DEFER

    def run(t, stages):
        for fn, lag in stages:
            @pl.when((t >= lag) & (t < nq + lag))
            def _():
                fn(t - lag)

    def early(t):
        @pl.when(t + AHEAD_Z < nq)
        def _():
            stage0z(t + AHEAD_Z)

        @pl.when(t + AHEAD_Y < nq)
        def _():
            stage0y(t + AHEAD_Y)
        for fn, lag in gather + [(stage_in, LAG_C)]:
            @pl.when(t == TABLE + lag)
            def _():
                fn(None)
        run(t, gather)

    def back(t):
        run(t, reduce_a)

        @pl.when((t >= start_r + LAG_G) & (t < nq - DIRECT + start_r + LAG_G))
        def _():
            stage_g(t - start_r - LAG_G)

        @pl.when((t >= start_r + LAG_S) & (t < early_rows + start_r + LAG_S))
        def _():
            stage_s(t - start_r - LAG_S)

    def first(t, _):
        @pl.when(t < chunks)
        def _():
            up_copy(t).start()
            down_copy(t).start()
        early(t)
        run(t, [(stage_c, LAG_C)])
        return 0

    def middle(t, _):
        early(t)
        back(t)
        run(t, [(stage_c, LAG_C), (stage_d, start_r)])
        return 0

    def final(t, _):
        back(t)
        run(t, [(stage_d, start_r)])
        return 0

    lax.fori_loop(0, AHEAD_Z, lambda q, _: (stage0z(q), 0)[1], 0)
    lax.fori_loop(0, AHEAD_Y, lambda q, _: (stage0y(q), 0)[1], 0)
    expert_row = lax.broadcasted_iota(jnp.int32, (lanes, rows), 0)
    spread = jnp.zeros((lanes, rows), f32)
    for k in range(ids_ref.shape[0]):
        spread += jnp.where(expert_row == ids_ref[k:k + 1, :], weights_ref[k:k + 1, :].astype(f32), 0.0)
    unit = (lax.broadcasted_iota(jnp.int32, (rows, rows), 0) == lax.broadcasted_iota(jnp.int32, (rows, rows), 1))
    table = lax.dot_general(
        unit.astype(f32).astype(jnp.bfloat16), spread.astype(jnp.bfloat16), (((1,), (1,)), ((), ())),
        preferred_element_type=f32).astype(wg.dtype)
    for h in range(2):
        wg[h, 0, rel(0), :] = table[h * hr:(h + 1) * hr, :]

    stage0z(None)
    stage0y(None)
    for h in range(2):
        own_x[h].wait()
    lax.fori_loop(0, start_r, first, 0)
    lax.fori_loop(start_r, nq + LAG_C, middle, 0)
    lax.fori_loop(nq + LAG_C, nq + late, final, 0)

    def whole(sem, blocks):
        while blocks:
            n = min(blocks, 4 * chunks)
            r = n if n < 4 else n - n % 4
            if n < 4:
                ref = xg.at[0, pl.ds(0, 1), pl.ds(0, hr), pl.ds(0, n * width)]
            else:
                ref = xg.at[0, pl.ds(0, 1), pl.ds(0, col), pl.ds(0, r // 4 * width)]
            sent(sem, ref)
            blocks -= r

    whole(gy_s.at[1, 0], nq)
    whole(gy_s.at[0, 0], nq * last)
    whole(gp_s.at[0], nq * 2 * major)
    for slot in range(4):
        @pl.when((*has, jnp.logical_not(corner))[slot])
        def _():
            whole(gz_s.at[slot, 0], nq)
            sent(gz_s.at[slot, 1], wg.at[:, 0, rel(0), :])
    sent(gy_s.at[1, 1], wg.at[:, 0, rel(0), :])
    sent(gy_s.at[0, 1], wg.at[:, 0, rel(1, last), :])
    sent(gp_s.at[1], wg.at[:, pl.ds(0, 2), :, :])
    whole(rp_s.at[0], nq * 2 * major)
    whole(ry_s.at[0], nq * last)
    lax.fori_loop(early_rows, nq, lambda r, _: (stage_s(r), 0)[1], 0)
    whole(ro_s.at[0], nq)
    for slot in range(4):
        @pl.when((*has, corner)[slot])
        def _():
            whole(rz_s.at[slot], nq)


def fused(tokens, expert_ids, route_weights, w_up, w_down, width=512):
    rows, depth = tokens.shape
    ff = w_up.shape[2]
    experts = lax.axis_size(("node", "local"))
    major = lax.axis_size("local") // 2
    chunks = depth // width
    lanes = -(-experts // LANES) * LANES
    col = major * rows // 2
    bf, f32 = jnp.bfloat16, jnp.float32
    nq = 2 * chunks
    dma = pltpu.SemaphoreType.DMA
    return pl.pallas_call(
        functools.partial(moe_kernel, (rows, major, chunks, width)),
        out_shape=pltpu.VMEM((rows, depth), bf),
        in_specs=[
            pl.BlockSpec(memory_space=pl.ANY),
            pl.BlockSpec(memory_space=pltpu.VMEM),
            pl.BlockSpec(memory_space=pltpu.VMEM),
            pl.BlockSpec(memory_space=pl.ANY),
            pl.BlockSpec(memory_space=pl.ANY),
        ],
        out_specs=pl.BlockSpec(memory_space=pltpu.VMEM),
        scratch_shapes=[
            pltpu.VMEM((2, 4, col, depth), bf),
            pltpu.VMEM((2, 4, col, lanes), bf),
            pltpu.VMEM((depth, ff), bf),
            pltpu.VMEM((ff, depth), bf),
            pltpu.VMEM((4 * col, ff), f32),
            pltpu.VMEM((2, 4 * col, ff), bf),
            pltpu.VMEM((2, 2, col, depth), bf),
            pltpu.VMEM((2, 2, col, depth), bf),
            pltpu.VMEM((2, 2, col, depth), f32),
            pltpu.VMEM((2, col, depth), bf),
            pltpu.VMEM((2, col, depth), bf),
            pltpu.VMEM((2, col, depth), bf),
            pltpu.VMEM((4, 2, rows // 2, depth), bf),
            dma((2,)), dma((chunks,)),
            dma((4, 2)), dma((3, nq + 1)),
            dma((2, 2)), dma((nq + 1,)),
            dma((2,)), dma((nq + 1,)),
            dma((1,)), dma((nq,)),
            dma((1,)), dma((nq,)),
            dma((1,)), dma((nq,)),
            dma((4,)), dma((2, nq)),
        ],
        compiler_params=pltpu.CompilerParams(
            collective_id=0, has_side_effects=True, vmem_limit_bytes=60 * 1024 * 1024),
    )(tokens, expert_ids.T, route_weights.T, w_up, w_down)


def place_rows(targets, groups, width):
    onehot = (targets[:, None] == jnp.arange(groups, dtype=jnp.int32)[None, :]).astype(jnp.int32)
    before = jnp.cumsum(onehot, axis=0) - onehot
    rank = jnp.sum(before * onehot, axis=1)
    return jnp.where(targets >= 0, targets * width + rank, groups * width)


def per_device(tokens, expert_ids, route_weights, w_up, w_down):
    up_matrix = w_up[0]
    down_matrix = w_down[0]
    rows = tokens.shape[0]
    top = expert_ids.shape[1]
    width_d = tokens.shape[1]
    experts = lax.axis_size(("node", "local"))
    most = max(4, 2 * rows * top // experts)
    slot = place_rows(expert_ids.reshape(-1), experts, most)
    source = tokens[jnp.arange(rows * top, dtype=jnp.int32) // top]
    buffer = jnp.zeros((experts * most, width_d), jnp.bfloat16).at[slot].set(source, mode="drop")
    buffer = buffer.reshape(experts, most, width_d)
    received = lax.all_to_all(buffer, ("node", "local"), split_axis=0, concat_axis=0, tiled=True)
    shape = received.shape
    flat = received.reshape(-1, shape[-1])
    hidden = jax.nn.silu(jnp.dot(flat, up_matrix, preferred_element_type=jnp.float32)).astype(
        jnp.bfloat16
    )
    answer = jnp.dot(hidden, down_matrix, preferred_element_type=jnp.float32).astype(jnp.bfloat16)
    done = answer.reshape(shape)
    returned = lax.all_to_all(
        done, ("node", "local"), split_axis=0, concat_axis=0, tiled=True
    ).reshape(experts * most, width_d)
    picked = returned[jnp.minimum(slot, experts * most - 1)].reshape(rows, top, width_d)
    mixed = jnp.einsum("tk,tkd->td", route_weights, picked, preferred_element_type=jnp.float32)
    return mixed.astype(jnp.bfloat16)


def solution(mesh):
    placed = (
        P(("rep", "node", "local"), None),
        P(("rep", "node", "local"), None),
        P(("rep", "node", "local"), None),
        P(("node", "local"), None, None),
        P(("node", "local"), None, None),
    )

    def body(tokens, expert_ids, route_weights, w_up, w_down):
        experts = mesh.shape["node"] * mesh.shape["local"]
        near_dense = experts <= 2 * expert_ids.shape[1]
        if near_dense and mesh.shape["node"] == 2 and mesh.shape["local"] == 8:
            return fused(tokens, expert_ids, route_weights, w_up, w_down)
        return per_device(tokens, expert_ids, route_weights, w_up, w_down)

    return jax.shard_map(
        body,
        mesh=mesh,
        in_specs=placed,
        out_specs=P(("rep", "node", "local"), None),
        check_vma=False,
    )
```

```python
import functools
import jax
import jax.numpy as jnp
from jax import lax
from jax.experimental import pallas as pl
from jax.experimental.pallas import tpu as pltpu
from jax.sharding import PartitionSpec as P

MESH = pl.DeviceIdType.MESH
LANES = 128
AHEAD_Z = 3
AHEAD_Y = 7
TABLE = 3
LAG_A = (1, 1, 3)
LAG_P = (4, 6)
LAG_C = 7
LAG_E = 2
LAG_F = 5
LAG_G = 8
LAG_S = 11
DEFER = 14
DIRECT = 2


def moe_kernel(sizes, x_hbm, ids_ref, weights_ref, up_hbm, down_hbm, out_ref,
               xg, wg, up, down, acc, hid, psend, precv, pown, ysend, yrecv, zs, zr,
               own_sem, up_sem,
               gz_s, gz_r, gy_s, gy_r, gp_s, gp_r,
               rp_s, rp_r, ry_s, ry_r, ro_s, ro_r, rz_s, rz_r):
    rows, major, chunks, width = sizes
    core = lax.axis_index("node")
    local = lax.axis_index("local")
    z, y = local // 2, lax.rem(local, 2)
    last = major - 1
    hr = rows // 2
    col = major * hr
    half = 2 * col
    grp = 2 * half
    nq = 2 * chunks
    f32 = jnp.float32

    up_z, down_z = jnp.minimum(z + 1, last), jnp.maximum(z - 1, 0)
    cross = lax.rem(z + 2, major)
    corner = (z == 0) | (z == last)
    far = jnp.where(corner, last - z, cross)
    nexts = tuple({"local": zz * 2 + y} for zz in (up_z, down_z, cross, far))
    inward = {"local": jnp.where(z == 0, 1, last - 1) * 2 + y}
    outward = {"local": jnp.where(z == 1, 0, last) * 2 + y}
    at_y = {"local": z * 2 + (1 - y)}
    at_p = {"node": 1 - core}
    has = (z < last, z > 0, z >= 0)
    came = (z > 0, z < last, z >= 0, corner)
    from_rel = (last, 1, 2, jnp.where(z == 0, last, 1))
    to_rel = (1, last, 2, jnp.where(z == 0, last, 1))
    lane_of = (0, 0, 1, 2)
    relay_rel = jnp.where(z == 1, last, 1)

    barrier = pltpu.get_barrier_semaphore()
    peers = [{"local": lax.rem(z + d, major) * 2 + y} for d in range(1, major)] + [at_y, at_p]
    for peer in peers:
        pl.semaphore_signal(barrier, inc=1, device_id=peer, device_id_type=MESH)

    def rel(k, n=1):
        return pl.ds(k * hr if isinstance(k, int) else pl.multiple_of(k * hr, hr), n * hr)

    own_x = []
    for h in range(2):
        own_x.append(pltpu.make_async_copy(
            x_hbm.at[pl.ds(h * hr, hr), :], xg.at[h, 0, rel(0), :], own_sem.at[h]))
        own_x[h].start()

    def cols(j):
        return pl.ds(pl.multiple_of(j * width, width), width)

    def up_copy(j):
        return pltpu.make_async_copy(up_hbm.at[0, cols(j), :], up.at[cols(j), :], up_sem.at[j])

    def down_copy(j):
        return pltpu.make_async_copy(down_hbm.at[0, :, cols(j)], down.at[:, cols(j)], up_sem.at[j])

    pl.semaphore_wait(barrier, len(peers))

    def split(q):
        h = (q >= chunks).astype(jnp.int32)
        return h, q - h * chunks

    def region(q, a, n, k, m):
        if q is None:
            return wg.at[:, pl.ds(a, n), rel(k, m), :]
        h, j = split(q)
        return xg.at[h, pl.ds(a, n), rel(k, m), cols(j)]

    def idx(q):
        return nq if q is None else q

    def kind(q):
        return 1 if q is None else 0

    def remote(src, dst, s, r, device):
        return pltpu.make_async_remote_copy(
            src_ref=src, dst_ref=dst, send_sem=s, recv_sem=r, device_id=device, device_id_type=MESH)

    def sent(sem, ref):
        remote(ref, ref, sem, sem, at_p).wait_send()

    def own(q, a, k):
        if q is None:
            return wg.at[:, 0, rel(0), :], wg.at[:, a, rel(k), :]
        h, j = split(q)
        return x_hbm.at[pl.ds(pl.multiple_of(h * hr, hr), hr), cols(j)], xg.at[h, a, rel(k), cols(j)]

    def gz(slot, q):
        return remote(*own(q, 0, from_rel[slot]), gz_s.at[slot, kind(q)], gz_r.at[lane_of[slot], idx(q)], nexts[slot])

    def relay(q):
        return remote(region(q, 0, 1, 2, 1), region(q, 0, 1, relay_rel, 1),
                      gz_s.at[3, kind(q)], gz_r.at[2, idx(q)], outward)

    def gz_in(lane, blocks, q):
        v = region(q, 0, 1, (1, 2, from_rel[3])[lane], blocks)
        return remote(v, v, gz_s.at[2, kind(q)], gz_r.at[lane, idx(q)], nexts[2])

    def gy(k, q):
        v = own(q, 1, 0) if k is None else (region(q, 0, 1, k, 1), region(q, 1, 1, k, 1))
        return remote(*v, gy_s.at[int(k is None), kind(q)], gy_r.at[idx(q)], at_y)

    def gy_in(q):
        v = region(q, 1, 1, 0, major)
        return remote(v, v, gy_s.at[0, kind(q)], gy_r.at[idx(q)], at_y)

    def gp(k, q):
        return remote(region(q, k, 1, 0, major), region(q, 2 + k, 1, 0, major), gp_s.at[kind(q)], gp_r.at[idx(q)], at_p)

    def gp_in(q):
        v = region(q, 2, 2, 0, major)
        return remote(v, v, gp_s.at[kind(q)], gp_r.at[idx(q)], at_p)

    def stage0z(q):
        for d in range(2):
            @pl.when(has[d])
            def _():
                gz(d, q).start()
        gz(2, q).start()

    def stage0y(q):
        gy(None, q).start()

    def stage_a(lane, q):
        if lane == 0:
            @pl.when(corner)
            def _():
                gz_in(0, 1, q).wait_recv()
                gy(jnp.where(z == 0, 1, last), q).start()

            @pl.when(jnp.logical_not(corner))
            def _():
                gz_in(0, 2, q).wait_recv()
                gy(1, q).start()
                gy(last, q).start()
        elif lane == 1:
            gz_in(1, 1, q).wait_recv()

            @pl.when(jnp.logical_not(corner))
            def _():
                relay(q).start()
            gy(2, q).start()
        else:
            @pl.when(corner)
            def _():
                gz_in(2, 1, q).wait_recv()
                gy(from_rel[3], q).start()

    def stage_p(k, q):
        if k == 1:
            gy_in(q).wait_recv()
        gp(k, q).start()

    def stage_in(q):
        gp_in(q).wait_recv()

    lanes = wg.shape[3]
    expert = core * (2 * major) + local

    def stage_c(q):
        stage_in(q)
        h, j = split(q)

        @pl.when(h == 0)
        def _():
            both = up.at[pl.ds(0, 2 * width), :]
            pltpu.make_async_copy(both, both, up_sem.at[j]).wait()
        x = xg[h, :, :, cols(j)].reshape(grp, width)
        part = jnp.dot(x, up[cols(j), :], preferred_element_type=f32)

        @pl.when(j == 0)
        def _():
            acc[...] = part

        @pl.when(j > 0)
        def _():
            acc[...] += part

        @pl.when(j == chunks - 1)
        def _():
            lane = lax.broadcasted_iota(jnp.int32, (grp, lanes), 1)
            table = wg[h].reshape(grp, lanes).astype(f32)
            weight = jnp.sum(jnp.where(lane == expert, table, 0.0), axis=1, keepdims=True)
            v = acc[...]
            hid[h] = (v / (1.0 + jnp.exp(-v)) * weight).astype(hid.dtype)

    def rp(r):
        h, j = split(r)
        return remote(psend.at[h, :, :, cols(j)], precv.at[h, :, :, cols(j)], rp_s.at[0], rp_r.at[r], at_p)

    def ry(r):
        h, j = split(r)
        v = (h, rel(1, last), cols(j))
        return remote(ysend.at[v], yrecv.at[v], ry_s.at[0], ry_r.at[r], at_y)

    def ro(r):
        h, j = split(r)
        v = (h, rel(0), cols(j))
        return remote(ysend.at[v], yrecv.at[v], ro_s.at[0], ro_r.at[r], at_y)

    def rz(slot, r):
        h, j = split(r)
        return remote(zs.at[h, rel(to_rel[slot]), cols(j)], zr.at[slot, h, :, cols(j)],
                      rz_s.at[slot], rz_r.at[0, r], nexts[slot])

    def rr(r):
        h, j = split(r)
        return remote(zs.at[h, rel(to_rel[3]), cols(j)], zr.at[3, h, :, cols(j)], rz_s.at[3], rz_r.at[1, r], inward)

    def stage_d(r):
        h, j = split(r)

        part = jnp.dot(hid[h], down[:, cols(j)], preferred_element_type=f32)
        psend[h, :, :, cols(j)] = part[half:, :].astype(psend.dtype).reshape(2, col, width)
        rp(r).start()
        pown[h, :, :, cols(j)] = part[:half, :].reshape(2, col, width)

    def stage_e(r):
        h, j = split(r)
        rp(r).wait_recv()
        ysend[h, :, cols(j)] = (pown[h, 1, :, cols(j)] + precv[h, 1, :, cols(j)].astype(f32)).astype(ysend.dtype)
        ry(r).start()

        @pl.when(r < nq - DEFER)
        def _():
            ro(r).start()
        pown[h, 0, :, cols(j)] += precv[h, 0, :, cols(j)].astype(f32)

        @pl.when(r == nq - 1)
        def _():
            lax.fori_loop(nq - DEFER, nq, lambda k, _: (ro(k).start(), 0)[1], 0)

    def stage_f(r):
        h, j = split(r)
        ry(r).wait_recv()
        v = (h, rel(1, last), cols(j))
        zs[v] = (pown[h, 0, rel(1, last), cols(j)] + yrecv[v].astype(f32)).astype(zs.dtype)

        by_hand = r < nq - DIRECT

        @pl.when(corner & by_hand)
        def _():
            rr(r).start()

        @pl.when(corner & jnp.logical_not(by_hand))
        def _():
            rz(3, r).start()

        @pl.when(corner | jnp.logical_not(by_hand))
        def _():
            rz(2, r).start()
        for slot in range(2):
            @pl.when(has[slot])
            def _():
                rz(slot, r).start()

    def stage_g(r):
        h, j = split(r)

        @pl.when(jnp.logical_not(corner))
        def _():
            rr(r).wait_recv()
            v = (h, rel(2), cols(j))
            zs[v] = (pown[h, 0, rel(2), cols(j)] + yrecv[v].astype(f32) + zr[3, h, :, cols(j)].astype(f32)).astype(zs.dtype)
            rz(2, r).start()

    def stage_s(r):
        h, j = split(r)
        ro(r).wait_recv()
        v = (h, 0, rel(0), cols(j))
        pown[v] += yrecv[h, rel(0), cols(j)].astype(f32)
        def arrived(n):
            blocks = zr.at[pl.ds(0, n), h, :, cols(j)]
            remote(blocks, blocks, rz_s.at[0], rz_r.at[0, r], nexts[2]).wait_recv()

        two = corner & (r < nq - DIRECT)
        pl.when(two)(lambda: arrived(2))
        pl.when(jnp.logical_not(two))(lambda: arrived(3))
        for slot in range(4):
            @pl.when(came[slot] & (r >= nq - DIRECT) if slot == 3 else came[slot])
            def _():
                pown[v] += zr[slot, h, :, cols(j)].astype(f32)
        out_ref[pl.ds(pl.multiple_of(h * hr, hr), hr), cols(j)] = pown[v].astype(out_ref.dtype)

    gather = [(functools.partial(stage_a, s), lag) for s, lag in zip(range(3), LAG_A)]
    gather += [(functools.partial(stage_p, k), LAG_P[k]) for k in range(2)]
    start_r = LAG_C + chunks - 1
    reduce_a = [(stage_e, start_r + LAG_E), (stage_f, start_r + LAG_F)]
    late = start_r + max(LAG_F, LAG_G - DIRECT, LAG_S - DEFER)
    early_rows = nq - DEFER

    def run(t, stages):
        for fn, lag in stages:
            @pl.when((t >= lag) & (t < nq + lag))
            def _():
                fn(t - lag)

    def early(t):
        @pl.when(t + AHEAD_Z < nq)
        def _():
            stage0z(t + AHEAD_Z)

        @pl.when(t + AHEAD_Y < nq)
        def _():
            stage0y(t + AHEAD_Y)
        for fn, lag in gather + [(stage_in, LAG_C)]:
            @pl.when(t == TABLE + lag)
            def _():
                fn(None)
        run(t, gather)

    def back(t):
        @pl.when((t >= start_r + LAG_G) & (t < nq - DIRECT + start_r + LAG_G))
        def _():
            stage_g(t - start_r - LAG_G)
        run(t, reduce_a)

        @pl.when((t >= start_r + LAG_S) & (t < early_rows + start_r + LAG_S))
        def _():
            stage_s(t - start_r - LAG_S)

    def first(t, _):
        @pl.when(t < chunks)
        def _():
            up_copy(t).start()
            down_copy(t).start()
        early(t)
        run(t, [(stage_c, LAG_C)])
        return 0

    def middle(t, _):
        early(t)
        back(t)
        run(t, [(stage_c, LAG_C), (stage_d, start_r)])
        return 0

    def final(t, _):
        back(t)
        run(t, [(stage_d, start_r)])
        return 0

    lax.fori_loop(0, AHEAD_Z, lambda q, _: (stage0z(q), 0)[1], 0)
    lax.fori_loop(0, AHEAD_Y, lambda q, _: (stage0y(q), 0)[1], 0)
    expert_row = lax.broadcasted_iota(jnp.int32, (lanes, rows), 0)
    spread = jnp.zeros((lanes, rows), f32)
    for k in range(ids_ref.shape[0]):
        spread += jnp.where(expert_row == ids_ref[k:k + 1, :], weights_ref[k:k + 1, :].astype(f32), 0.0)
    unit = (lax.broadcasted_iota(jnp.int32, (rows, rows), 0) == lax.broadcasted_iota(jnp.int32, (rows, rows), 1))
    table = lax.dot_general(
        unit.astype(f32).astype(jnp.bfloat16), spread.astype(jnp.bfloat16), (((1,), (1,)), ((), ())),
        preferred_element_type=f32).astype(wg.dtype)
    for h in range(2):
        wg[h, 0, rel(0), :] = table[h * hr:(h + 1) * hr, :]

    stage0z(None)
    stage0y(None)
    for h in range(2):
        own_x[h].wait()
    lax.fori_loop(0, start_r, first, 0)
    lax.fori_loop(start_r, nq + LAG_C, middle, 0)
    lax.fori_loop(nq + LAG_C, nq + late, final, 0)

    def whole(sem, blocks):
        while blocks:
            n = min(blocks, 4 * chunks)
            r = n if n < 4 else n - n % 4
            if n < 4:
                ref = xg.at[0, pl.ds(0, 1), pl.ds(0, hr), pl.ds(0, n * width)]
            else:
                ref = xg.at[0, pl.ds(0, 1), pl.ds(0, col), pl.ds(0, r // 4 * width)]
            sent(sem, ref)
            blocks -= r

    whole(gy_s.at[1, 0], nq)
    whole(gy_s.at[0, 0], nq * last)
    whole(gp_s.at[0], nq * 2 * major)
    for slot in range(4):
        @pl.when((*has, jnp.logical_not(corner))[slot])
        def _():
            whole(gz_s.at[slot, 0], nq)
            sent(gz_s.at[slot, 1], wg.at[:, 0, rel(0), :])
    sent(gy_s.at[1, 1], wg.at[:, 0, rel(0), :])
    sent(gy_s.at[0, 1], wg.at[:, 0, rel(1, last), :])
    sent(gp_s.at[1], wg.at[:, pl.ds(0, 2), :, :])
    whole(rp_s.at[0], nq * 2 * major)
    whole(ry_s.at[0], nq * last)
    lax.fori_loop(early_rows, nq, lambda r, _: (stage_s(r), 0)[1], 0)
    whole(ro_s.at[0], nq)
    for slot in range(4):
        @pl.when((*has, corner)[slot])
        def _():
            whole(rz_s.at[slot], nq)


def fused(tokens, expert_ids, route_weights, w_up, w_down, width=512):
    rows, depth = tokens.shape
    ff = w_up.shape[2]
    experts = lax.axis_size(("node", "local"))
    major = lax.axis_size("local") // 2
    chunks = depth // width
    lanes = -(-experts // LANES) * LANES
    col = major * rows // 2
    bf, f32 = jnp.bfloat16, jnp.float32
    nq = 2 * chunks
    dma = pltpu.SemaphoreType.DMA
    return pl.pallas_call(
        functools.partial(moe_kernel, (rows, major, chunks, width)),
        out_shape=pltpu.VMEM((rows, depth), bf),
        in_specs=[
            pl.BlockSpec(memory_space=pl.ANY),
            pl.BlockSpec(memory_space=pltpu.VMEM),
            pl.BlockSpec(memory_space=pltpu.VMEM),
            pl.BlockSpec(memory_space=pl.ANY),
            pl.BlockSpec(memory_space=pl.ANY),
        ],
        out_specs=pl.BlockSpec(memory_space=pltpu.VMEM),
        scratch_shapes=[
            pltpu.VMEM((2, 4, col, depth), bf),
            pltpu.VMEM((2, 4, col, lanes), bf),
            pltpu.VMEM((depth, ff), bf),
            pltpu.VMEM((ff, depth), bf),
            pltpu.VMEM((4 * col, ff), f32),
            pltpu.VMEM((2, 4 * col, ff), bf),
            pltpu.VMEM((2, 2, col, depth), bf),
            pltpu.VMEM((2, 2, col, depth), bf),
            pltpu.VMEM((2, 2, col, depth), f32),
            pltpu.VMEM((2, col, depth), bf),
            pltpu.VMEM((2, col, depth), bf),
            pltpu.VMEM((2, col, depth), bf),
            pltpu.VMEM((4, 2, rows // 2, depth), bf),
            dma((2,)), dma((chunks,)),
            dma((4, 2)), dma((3, nq + 1)),
            dma((2, 2)), dma((nq + 1,)),
            dma((2,)), dma((nq + 1,)),
            dma((1,)), dma((nq,)),
            dma((1,)), dma((nq,)),
            dma((1,)), dma((nq,)),
            dma((4,)), dma((2, nq)),
        ],
        compiler_params=pltpu.CompilerParams(
            collective_id=0, has_side_effects=True, vmem_limit_bytes=60 * 1024 * 1024),
    )(tokens, expert_ids.T, route_weights.T, w_up, w_down)


def place_rows(targets, groups, width):
    onehot = (targets[:, None] == jnp.arange(groups, dtype=jnp.int32)[None, :]).astype(jnp.int32)
    before = jnp.cumsum(onehot, axis=0) - onehot
    rank = jnp.sum(before * onehot, axis=1)
    return jnp.where(targets >= 0, targets * width + rank, groups * width)


def per_device(tokens, expert_ids, route_weights, w_up, w_down):
    up_matrix = w_up[0]
    down_matrix = w_down[0]
    rows = tokens.shape[0]
    top = expert_ids.shape[1]
    width_d = tokens.shape[1]
    experts = lax.axis_size(("node", "local"))
    most = max(4, 2 * rows * top // experts)
    slot = place_rows(expert_ids.reshape(-1), experts, most)
    source = tokens[jnp.arange(rows * top, dtype=jnp.int32) // top]
    buffer = jnp.zeros((experts * most, width_d), jnp.bfloat16).at[slot].set(source, mode="drop")
    buffer = buffer.reshape(experts, most, width_d)
    received = lax.all_to_all(buffer, ("node", "local"), split_axis=0, concat_axis=0, tiled=True)
    shape = received.shape
    flat = received.reshape(-1, shape[-1])
    hidden = jax.nn.silu(jnp.dot(flat, up_matrix, preferred_element_type=jnp.float32)).astype(
        jnp.bfloat16
    )
    answer = jnp.dot(hidden, down_matrix, preferred_element_type=jnp.float32).astype(jnp.bfloat16)
    done = answer.reshape(shape)
    returned = lax.all_to_all(
        done, ("node", "local"), split_axis=0, concat_axis=0, tiled=True
    ).reshape(experts * most, width_d)
    picked = returned[jnp.minimum(slot, experts * most - 1)].reshape(rows, top, width_d)
    mixed = jnp.einsum("tk,tkd->td", route_weights, picked, preferred_element_type=jnp.float32)
    return mixed.astype(jnp.bfloat16)


def solution(mesh):
    placed = (
        P(("rep", "node", "local"), None),
        P(("rep", "node", "local"), None),
        P(("rep", "node", "local"), None),
        P(("node", "local"), None, None),
        P(("node", "local"), None, None),
    )

    def body(tokens, expert_ids, route_weights, w_up, w_down):
        experts = mesh.shape["node"] * mesh.shape["local"]
        near_dense = experts <= 2 * expert_ids.shape[1]
        if near_dense and mesh.shape["node"] == 2 and mesh.shape["local"] == 8:
            return fused(tokens, expert_ids, route_weights, w_up, w_down)
        return per_device(tokens, expert_ids, route_weights, w_up, w_down)

    return jax.shard_map(
        body,
        mesh=mesh,
        in_specs=placed,
        out_specs=P(("rep", "node", "local"), None),
        check_vma=False,
    )
```
